32 devices in a mesh: py: 4 (over y, x), px: 8 (over z, core).
Axes of the slice: x: 2, y: 2, z: 4, core: 2. Of those that a mesh axis runs over, the one named last changes fastest.
Arguments:
- movie: bfloat16 [256, 128, 2048], P('py', 'px'), may hold values from -6 to 6
- traces: bfloat16 [4096, 2048], P('py', 'px'), may hold values from -0.125 to 0.125
- footprints: float32 [256, 128, 512], P('py', 'px'), may hold values from 0 to 1
- block_ids: int32 [4, 8, 4], P('py', 'px'), may hold values from 0 to 32, as said below
Outputs:
- updated: float32 [256, 128, 512], P('py', 'px')
The draws below stay inside these ranges and needn't reach their ends.
Inputs may be any that keep to these rules, and one draw needn't show every extreme that they name: `block_ids`: in each tile's list of 4 entries the live entries come first and are distinct block numbers below 32; the remaining entries equal 32 and mark empty slots. Every tile has at least one live entry, and some tile has all 4 live.
All inputs are finite; a program needn't handle non-finite values.
Results may differ from the reference program's by a relative error of at most 0.0003.
Values may be sent and summed in bfloat16 or wider, within the bound.
A program may use at most 64 MiB of HBM per device.

```python
import jax
import jax.numpy as jnp
from jax import lax

K = 4096
BLK = 128
SLOTS = 4
ITERS = 2
FRAMES = 2048
ROWS_DEV = 64
COLS_DEV = 16
NBLK = 32
NR = 256
NC = 128
TROWS = 4
TCOLS = 8
N_PY = 4
N_PX = 8


def draw_block_ids(key, part):
    base = jax.random.fold_in(key, 11)
    key_score, key_count, key_full = jax.random.split(base, 3)
    tiles = TROWS * TCOLS
    scores = jax.random.randint(key_score, (tiles, NBLK), 0, 2 ** 20) * NBLK + jnp.arange(NBLK, dtype=jnp.int32)[None, :]
    order = jnp.argsort(scores, axis=1)[:, :SLOTS].astype(jnp.int32)
    counts = jax.random.randint(key_count, (tiles,), 1, SLOTS + 1)
    fullest = jax.random.randint(key_full, (), 0, tiles)
    counts = jnp.where(jnp.arange(tiles) == fullest, SLOTS, counts)
    slot_index = jnp.arange(SLOTS, dtype=jnp.int32)[None, :]
    chosen = jnp.where(slot_index < counts[:, None], order, NBLK)
    return chosen.reshape(TROWS, TCOLS, SLOTS).astype(jnp.int32)


def shard_levels(stream_key, dims, shards, smallest, largest):
    level = 1.0
    for dim, blocks in shards:
        draws = jax.random.uniform(jax.random.fold_in(jax.random.fold_in(stream_key, 6), dim), (blocks,), jnp.float32, smallest / len(shards), largest / len(shards))
        level = level * jnp.repeat(jnp.exp(draws), dims[dim] // blocks).reshape((-1,) + (1,) * (len(dims) - 1 - dim))
    return level


def bell_draw(rng, shape, spread, reach, cuts=(), kind=jnp.bfloat16):
    drawn = jax.random.normal(rng, shape, jnp.float32) * spread
    if len(cuts) > 0:
        drawn = shard_levels(rng, shape, cuts, -0.22, 0.18) * drawn
    return jnp.clip(drawn, min=-reach, max=reach).astype(kind)


def setup_inputs(seed: int = 0) -> dict:
    arg_keys = jax.random.split(jax.random.key(seed), 5)
    return {
        "movie": bell_draw(arg_keys[0], (NR, NC, FRAMES), 1.0, 6.0, ((0, 4), (1, 8))),
        "traces": bell_draw(arg_keys[1], (K, FRAMES), FRAMES ** -0.5, 0.125, ((0, 4), (1, 8))),
        "footprints": jnp.clip(1.0 * jax.random.uniform(arg_keys[2], (NR, NC, SLOTS * BLK), jnp.float32) ** shard_levels(arg_keys[2], (NR, NC, SLOTS * BLK), ((0, 4), (1, 8)), -0.2, 0.2), 0.0, 1.0),
        "block_ids": draw_block_ids(jax.random.fold_in(arg_keys[4], 71), 0),
    }


def reference(movie, traces, footprints, block_ids):
    tiles = N_PY * N_PX
    pix = ROWS_DEV * COLS_DEV
    width = SLOTS * BLK
    nblk = K // BLK
    ytiles = movie.reshape(N_PY, ROWS_DEV, N_PX, COLS_DEV, FRAMES).transpose(0, 2, 1, 3, 4).reshape(tiles, pix, FRAMES)
    atiles = footprints.reshape(N_PY, ROWS_DEV, N_PX, COLS_DEV, width).transpose(0, 2, 1, 3, 4).reshape(tiles, pix, width)
    ids = block_ids.reshape(tiles, SLOTS)
    onehot = (ids[:, :, None] == jnp.arange(nblk, dtype=jnp.int32)[None, None, :]).astype(jnp.float32)
    live = lax.optimization_barrier(jnp.sum(onehot, axis=2))
    blocks = traces.reshape(nblk, BLK, FRAMES).astype(jnp.float32)
    gram_all = jnp.dot(traces, traces.T, preferred_element_type=jnp.float32).reshape(nblk, BLK, nblk, BLK)

    def per_tile(args):
        tile_movie, hot = args
        picked = jnp.einsum('sb,bnf->snf', hot, blocks).astype(jnp.bfloat16).reshape(width, FRAMES)
        cross = jnp.dot(tile_movie, picked.T, preferred_element_type=jnp.float32)
        gram = jnp.einsum('sb,bncq,dc->sndq', hot, gram_all, hot, precision=lax.Precision.HIGHEST).reshape(width, width)
        return (cross, gram)
    cross, gram = lax.map(per_tile, (ytiles, onehot))
    column_live = jnp.repeat(live, BLK, axis=1)
    denom = jnp.diagonal(gram, axis1=1, axis2=2) + 1e-06 + (1.0 - column_live)
    current = atiles * column_live[:, None, :]
    pixall = NR * NC
    for step in range(ITERS):
        for slot in range(SLOTS):
            low = slot * BLK
            columns = gram[:, :, low:low + BLK]
            resid = cross[:, :, low:low + BLK] - jnp.einsum('tpk,tkn->tpn', current, columns, precision=lax.Precision.HIGHEST)
            fresh = jnp.maximum(current[:, :, low:low + BLK] + resid / denom[:, None, low:low + BLK], 0.0)
            current = current.at[:, :, low:low + BLK].set(fresh)
        colsq = lax.optimization_barrier(jnp.sum(current * current, axis=1)).reshape(tiles, SLOTS, BLK)
        totals = jnp.einsum('tsb,tsn->bn', onehot, colsq, precision=lax.Precision.HIGHEST)
        factor = 1.0 / jnp.sqrt(totals / pixall + 1e-06)
        scale = jnp.einsum('tsb,bn->tsn', onehot, factor, precision=lax.Precision.HIGHEST).reshape(tiles, width)
        current = current * scale[:, None, :]
    return current.reshape(N_PY, N_PX, ROWS_DEV, COLS_DEV, width).transpose(0, 2, 1, 3, 4).reshape(NR, NC, width)
```

```python
import functools

import jax
import jax.numpy as jnp
from jax import lax
from jax.experimental import pallas as pl
from jax.experimental.pallas import tpu as pltpu
from jax.sharding import PartitionSpec as P

ITERS = 2
CHUNKS = 4
MESH = pl.DeviceIdType.MESH
BF = jnp.bfloat16
F32 = jnp.float32


def split(x):
    hi = x.astype(BF)
    return hi, (x - hi.astype(F32)).astype(BF)


def mm(a, b):
    return lax.dot_general(a, b, (((1,), (0,)), ((), ())), preferred_element_type=F32)


def kernel(
    n_py, n_px, movie, traces, foot, ids, cur_out, scale_out,
    y_buf, outb, recv, land, cur, crs, hilo, id_tile, id_all, id_smem, t_send, t_recv, live_row,
    local_sem, own_sem, id_ssem, id_rsem, g_ssem, g_rsem, x_ssem, x_rsem, t_ssem, t_rsem, *spans,
):
    py, px = lax.axis_index("py"), lax.axis_index("px")
    total = n_py * n_px
    me = py * n_px + px
    loc, blk, wid = traces.shape
    nblk = loc * n_py
    slots = recv.shape[0]
    width = slots * blk
    direct = wid % 128 == 0
    pixels = y_buf.shape[0]
    step_rows = blk // CHUNKS

    owns = [
        pltpu.make_async_copy(
            traces.at[:, pl.ds(c * step_rows, step_rows), :], spans[c].at[pl.ds(py * loc, loc)], own_sem.at[c]
        )
        for c in range(CHUNKS)
    ]
    for own in owns:
        own.start()
    get_foot = pltpu.make_async_copy(foot, cur, local_sem.at[1])
    get_movie = pltpu.make_async_copy(movie, y_buf, local_sem.at[2])

    sub = lax.broadcasted_iota(jnp.int32, (8, blk), 0)
    tile = jnp.zeros((8, blk), jnp.int32)
    for s in range(slots):
        tile = jnp.where(sub == 4 + s, ids[0, 0, s], tile)
    id_tile[...] = tile
    id_all[px] = tile
    for s in range(slots):
        alive = ((tile[4 + s : 5 + s, :] >= 0) & (tile[4 + s : 5 + s, :] < nblk)).astype(F32)
        live_row[:, s * blk : (s + 1) * blk] = alive

    barrier = pltpu.get_barrier_semaphore()

    def greet(k, _):
        dest = lax.rem(me + k, total)
        pl.semaphore_signal(
            barrier, inc=1, device_id={"py": dest // n_px, "px": lax.rem(dest, n_px)}, device_id_type=MESH
        )
        return _

    lax.fori_loop(1, total, greet, 0)
    pl.semaphore_wait(barrier, total - 1)

    def id_copy(k):
        return pltpu.make_async_remote_copy(
            src_ref=id_tile, dst_ref=id_all.at[px], send_sem=id_ssem.at[k], recv_sem=id_rsem.at[k],
            device_id={"px": lax.rem(px + k, n_px)}, device_id_type=MESH,
        )

    def gather_copy(c, k):
        rows = pl.ds(c * step_rows, step_rows)
        return pltpu.make_async_remote_copy(
            src_ref=traces.at[:, rows, :], dst_ref=spans[c].at[pl.ds(py * loc, loc)],
            send_sem=g_ssem.at[c, k], recv_sem=g_rsem.at[c, k],
            device_id={"py": lax.rem(py + k, n_py)}, device_id_type=MESH,
        )

    def x_copy(c, k):
        rows = pl.ds(c * step_rows, step_rows)
        dest = lax.rem(px + k, n_px)
        if direct:
            target = recv.at[:, rows, pl.ds(pl.multiple_of(px * wid, wid), wid)]
        else:
            target = land.at[px, :, rows, :]
        return pltpu.make_async_remote_copy(
            src_ref=outb.at[dest, :, rows, :],
            dst_ref=target,
            send_sem=x_ssem.at[c, k], recv_sem=x_rsem.at[c, k],
            device_id={"px": dest}, device_id_type=MESH,
        )

    def run(lo, hi, fn):
        def body(k, carry):
            fn(k)
            return carry

        lax.fori_loop(lo, hi, body, 0)

    run(1, n_px, lambda k: id_copy(k).start())
    for c in range(CHUNKS):
        run(1, n_py, lambda k: gather_copy(c, k).start())
    get_movie.start()
    get_foot.start()
    run(1, n_px, lambda k: id_copy(k).wait())
    to_smem = pltpu.make_async_copy(id_all, id_smem, local_sem.at[3])
    to_smem.start()
    to_smem.wait()

    def pick(dest, s, c):
        number = id_smem[dest, 4 + s, 0]
        ok = ((number >= 0) & (number < nblk)).astype(F32).astype(BF)
        index = jnp.minimum(jnp.maximum(number, 0), nblk - 1)
        return spans[c][index] * ok

    for c in range(CHUNKS):
        rows = pl.ds(c * step_rows, step_rows)
        owns[c].wait()
        run(1, n_py, lambda k: gather_copy(c, k).wait_recv())

        def route(k):
            dest = lax.rem(px + k, n_px)
            for s in range(slots):
                outb[dest, s, rows, :] = pick(dest, s, c)
            x_copy(c, k).start()

        run(1, n_px, route)
        for s in range(slots):
            if direct:
                recv[s, rows, pl.ds(pl.multiple_of(px * wid, wid), wid)] = pick(px, s, c)
            else:
                land[px, s, rows, :] = pick(px, s, c)

    get_foot.wait()
    get_movie.wait()
    for c in range(CHUNKS):
        run(1, n_px, lambda k: x_copy(c, k).wait_recv())
    if not direct:
        pack = blk // wid
        for q in range(n_px // pack):
            both = [land[q * pack + j] for j in range(pack)]
            recv[:, :, q * blk : (q + 1) * blk] = jnp.concatenate(both, axis=-1)

    mine = recv[...].reshape(width, recv.shape[2])
    gram = lax.dot_general(mine, mine, (((1,), (1,)), ((), ())), preferred_element_type=F32)
    eye = lax.broadcasted_iota(jnp.int32, (width, width), 0) == lax.broadcasted_iota(jnp.int32, (width, width), 1)
    live = live_row[...]
    denom = jnp.sum(jnp.where(eye, gram, 0.0), axis=0, keepdims=True) + 1e-06 + (1.0 - live)
    inv = 1.0 / denom
    hi, lo = split(jnp.where(eye, 1.0, 0.0) - gram * inv)
    for s in range(slots):
        hilo[s, :, :blk] = hi[:, s * blk : (s + 1) * blk]
        hilo[s, :, blk:] = lo[:, s * blk : (s + 1) * blk]
    part = min(pixels, 256)

    def cross_part(i):
        at = pl.ds(pl.multiple_of(i * part, part), part)
        prod = lax.dot_general(
            y_buf[at, :], recv[...].reshape(width, recv.shape[2]), (((1,), (1,)), ((), ())), preferred_element_type=F32
        )
        crs[at, :] = prod * inv
        cur[at, :] = cur[at, :] * live

    run(0, pixels // part, cross_part)

    def total_copy(step, k):
        dest = lax.rem(me + k, total)
        return pltpu.make_async_remote_copy(
            src_ref=t_send.at[step], dst_ref=t_recv.at[step, k - 1],
            send_sem=t_ssem.at[step], recv_sem=t_rsem.at[step],
            device_id={"py": dest // n_px, "px": lax.rem(dest, n_px)}, device_id_type=MESH,
        )

    ids_f = tile.astype(F32)
    scale = jnp.ones((1, width), F32)
    put = pltpu.make_async_copy(cur, cur_out, local_sem.at[4])
    for step in range(ITERS):

        def sweep(i, sums, scale=scale):
            at = pl.ds(pl.multiple_of(i * part, part), part)
            now = cur[at, :] * scale
            pieces = [now[:, s * blk : (s + 1) * blk] for s in range(slots)]
            his, los = zip(*[split(p) for p in pieces])
            his, los = list(his), list(los)
            squares = []
            for s in range(slots):
                m = hilo[s]
                wide = mm(jnp.concatenate(his, axis=1), m)
                thin = mm(jnp.concatenate(los, axis=1), m[:, :blk])
                fresh = jnp.maximum(
                    crs[at, s * blk : (s + 1) * blk] + (wide[:, :blk] + wide[:, blk:] + thin), 0.0
                )
                cur[at, s * blk : (s + 1) * blk] = fresh
                his[s], los[s] = split(fresh)
                squares.append(jnp.sum(fresh * fresh, axis=0, keepdims=True))
            return sums + jnp.concatenate(squares, axis=1)

        sums = lax.fori_loop(0, pixels // part, sweep, jnp.zeros((1, width), F32))
        mine_tile = ids_f
        for s in range(slots):
            mine_tile = jnp.where(sub == s, sums[:, s * blk : (s + 1) * blk], mine_tile)
        t_send[step] = mine_tile
        run(1, total, lambda k: total_copy(step, k).start())
        if step == ITERS - 1:
            put.start()
        pltpu.make_async_copy(t_recv.at[step], t_recv.at[step], t_rsem.at[step]).wait()
        got = t_recv[step]
        scales = []
        for s in range(slots):
            want = ids_f[4 + s : 5 + s, :]
            acc = sums[:, s * blk : (s + 1) * blk]
            same = jnp.where(got[:, 4 : 4 + slots, :] == want[None], got[:, :slots, :], 0.0)
            acc = acc + jnp.sum(jnp.sum(same, axis=0), axis=0, keepdims=True)
            scales.append(1.0 / jnp.sqrt(acc / (pixels * total) + 1e-06))
        scale = jnp.concatenate(scales, axis=1) * live
    scale_out[...] = jnp.broadcast_to(scale, scale_out.shape)

    put.wait()
    for c in range(CHUNKS):
        run(1, n_py, lambda k: gather_copy(c, k).wait_send())
        run(1, n_px, lambda k: x_copy(c, k).wait_send())
    for step in range(ITERS):
        pltpu.make_async_copy(t_recv.at[step], t_recv.at[step], t_ssem.at[step]).wait()


def per_device(n_py, n_px, movie, traces, footprints, block_ids):
    rows, cols, frames = movie.shape
    pixels = rows * cols
    width = footprints.shape[-1]
    slots = block_ids.shape[-1]
    blk = width // slots
    wid = traces.shape[1]
    loc = traces.shape[0] // blk
    total = n_py * n_px
    hbm = pl.BlockSpec(memory_space=pl.ANY)
    dma = pltpu.SemaphoreType.DMA
    current, scale = pl.pallas_call(
        functools.partial(kernel, n_py, n_px),
        out_shape=(
            jax.ShapeDtypeStruct((pixels, width), F32),
            jax.ShapeDtypeStruct((8, width), F32),
        ),
        in_specs=[hbm, hbm, hbm, pl.BlockSpec(memory_space=pltpu.SMEM)],
        out_specs=(hbm, pl.BlockSpec(memory_space=pltpu.VMEM)),
        scratch_shapes=[
            pltpu.VMEM((pixels, frames), BF),
            pltpu.VMEM((n_px, slots, blk, wid), BF),
            pltpu.VMEM((slots, blk, frames), BF),
            pltpu.VMEM((8, 128) if wid % 128 == 0 else (n_px, slots, blk, wid), BF),
            pltpu.VMEM((pixels, width), F32),
            pltpu.VMEM((pixels, width), F32),
            pltpu.VMEM((slots, width, 2 * blk), BF),
            pltpu.VMEM((8, blk), jnp.int32),
            pltpu.VMEM((n_px, 8, blk), jnp.int32),
            pltpu.SMEM((n_px, 8, blk), jnp.int32),
            pltpu.VMEM((ITERS, 8, blk), F32),
            pltpu.VMEM((ITERS, total - 1, 8, blk), F32),
            pltpu.VMEM((1, width), F32),
            dma((5,)), dma((CHUNKS,)),
            dma((n_px,)), dma((n_px,)),
            dma((CHUNKS, n_py)), dma((CHUNKS, n_py)),
            dma((CHUNKS, n_px)), dma((CHUNKS, n_px)),
            dma((ITERS,)), dma((ITERS,)),
            *[pltpu.VMEM((loc * n_py, blk // CHUNKS, wid), BF) for _ in range(CHUNKS)],
        ],
        compiler_params=pltpu.CompilerParams(
            collective_id=0, has_side_effects=True, vmem_limit_bytes=48 * 1024 * 1024
        ),
    )(
        movie.reshape(pixels, frames),
        traces.reshape(loc, blk, wid),
        footprints.reshape(pixels, width),
        block_ids,
    )
    return (current * scale[:1]).reshape(rows, cols, width)


def solution(mesh):
    return jax.shard_map(
        functools.partial(per_device, mesh.shape["py"], mesh.shape["px"]),
        mesh=mesh,
        in_specs=(P("py", "px", None), P("py", "px"), P("py", "px", None), P("py", "px", None)),
        out_specs=P("py", "px", None),
        check_vma=False,
    )
```

```python
import functools

import jax
import jax.numpy as jnp
from jax import lax
from jax.experimental import pallas as pl
from jax.experimental.pallas import tpu as pltpu
from jax.sharding import PartitionSpec as P

ITERS = 2
CHUNKS = 8
MESH = pl.DeviceIdType.MESH
BF = jnp.bfloat16
F32 = jnp.float32


def split(x):
    hi = x.astype(BF)
    return hi, (x - hi.astype(F32)).astype(BF)


def mm(a, b):
    return lax.dot_general(a, b, (((1,), (0,)), ((), ())), preferred_element_type=F32)


def kernel(
    n_py, n_px, movie, traces, foot, ids, cur_out, scale_out,
    y_buf, outb, recv, land, cur, crs, hilo, id_tile, id_all, id_smem, t_send, t_recv, live_row,
    local_sem, own_sem, id_ssem, id_rsem, g_ssem, g_rsem, x_ssem, x_rsem, t_ssem, t_rsem, *spans,
):
    py, px = lax.axis_index("py"), lax.axis_index("px")
    total = n_py * n_px
    me = py * n_px + px
    loc, blk, wid = traces.shape
    nblk = loc * n_py
    slots = recv.shape[0]
    width = slots * blk
    direct = wid % 128 == 0
    pixels = y_buf.shape[0]
    step_rows = blk // CHUNKS

    owns = [
        pltpu.make_async_copy(
            traces.at[:, pl.ds(c * step_rows, step_rows), :], spans[c].at[pl.ds(py * loc, loc)], own_sem.at[c]
        )
        for c in range(CHUNKS)
    ]
    for own in owns:
        own.start()
    get_foot = pltpu.make_async_copy(foot, cur, local_sem.at[1])
    get_movie = pltpu.make_async_copy(movie, y_buf, local_sem.at[2])

    sub = lax.broadcasted_iota(jnp.int32, (8, blk), 0)
    tile = jnp.zeros((8, blk), jnp.int32)
    for s in range(slots):
        tile = jnp.where(sub == 4 + s, ids[0, 0, s], tile)
    id_tile[...] = tile
    id_all[px] = tile
    for s in range(slots):
        alive = ((tile[4 + s : 5 + s, :] >= 0) & (tile[4 + s : 5 + s, :] < nblk)).astype(F32)
        live_row[:, s * blk : (s + 1) * blk] = alive

    barrier = pltpu.get_barrier_semaphore()

    def greet(k, _):
        dest = lax.rem(me + k, total)
        pl.semaphore_signal(
            barrier, inc=1, device_id={"py": dest // n_px, "px": lax.rem(dest, n_px)}, device_id_type=MESH
        )
        return _

    lax.fori_loop(1, total, greet, 0)
    pl.semaphore_wait(barrier, total - 1)

    def id_copy(k):
        return pltpu.make_async_remote_copy(
            src_ref=id_tile, dst_ref=id_all.at[px], send_sem=id_ssem.at[k], recv_sem=id_rsem.at[k],
            device_id={"px": lax.rem(px + k, n_px)}, device_id_type=MESH,
        )

    def gather_copy(c, k):
        rows = pl.ds(c * step_rows, step_rows)
        return pltpu.make_async_remote_copy(
            src_ref=traces.at[:, rows, :], dst_ref=spans[c].at[pl.ds(py * loc, loc)],
            send_sem=g_ssem.at[c, k], recv_sem=g_rsem.at[c, k],
            device_id={"py": lax.rem(py + k, n_py)}, device_id_type=MESH,
        )

    half = CHUNKS // 2
    pair = max(slots // 2, 1)
    pieces = [(c, 1, 0, slots) for c in range(half)]
    pieces += [(half, CHUNKS - half, s, pair) for s in range(0, slots, pair)]

    def x_copy(c, k):
        first, count, low, many = pieces[c]
        rows = pl.ds(first * step_rows, count * step_rows)
        group = pl.ds(low, many)
        dest = lax.rem(px + k, n_px)
        if direct:
            target = recv.at[group, rows, pl.ds(pl.multiple_of(px * wid, wid), wid)]
        else:
            target = land.at[px, group, rows, :]
        return pltpu.make_async_remote_copy(
            src_ref=outb.at[dest, group, rows, :],
            dst_ref=target,
            send_sem=x_ssem.at[c, k], recv_sem=x_rsem.at[c, k],
            device_id={"px": dest}, device_id_type=MESH,
        )

    def run(lo, hi, fn):
        def body(k, carry):
            fn(k)
            return carry

        lax.fori_loop(lo, hi, body, 0)

    run(1, n_px, lambda k: id_copy(k).start())
    for c in range(CHUNKS):
        run(1, n_py, lambda k: gather_copy(c, k).start())
    get_movie.start()
    get_foot.start()
    run(1, n_px, lambda k: id_copy(k).wait())
    to_smem = pltpu.make_async_copy(id_all, id_smem, local_sem.at[3])
    to_smem.start()
    to_smem.wait()

    def pick(dest, s, c):
        number = id_smem[dest, 4 + s, 0]
        ok = ((number >= 0) & (number < nblk)).astype(F32).astype(BF)
        index = jnp.minimum(jnp.maximum(number, 0), nblk - 1)
        return spans[c][index] * ok

    for c, (first, count, low, many) in enumerate(pieces):
        if low == 0:
            for g in range(first, first + count):
                owns[g].wait()
                run(1, n_py, lambda k: gather_copy(g, k).wait_recv())

        def route(k):
            dest = lax.rem(px + k, n_px)
            for g in range(first, first + count):
                for s in range(low, low + many):
                    outb[dest, s, pl.ds(g * step_rows, step_rows), :] = pick(dest, s, g)
            x_copy(c, k).start()

        run(1, n_px, route)
        for g in range(first, first + count):
            rows = pl.ds(g * step_rows, step_rows)
            for s in range(low, low + many):
                if direct:
                    recv[s, rows, pl.ds(pl.multiple_of(px * wid, wid), wid)] = pick(px, s, g)
                else:
                    land[px, s, rows, :] = pick(px, s, g)

    get_foot.wait()
    get_movie.wait()
    live = live_row[...]
    part = min(pixels, 256)
    frames = recv.shape[2]

    def cross_part(low, i):
        at = pl.ds(pl.multiple_of(i * part, part), part)
        cols = pl.ds(low * blk, pair * blk)
        crs[at, cols] = lax.dot_general(
            y_buf[at, :], recv[low : low + pair].reshape(pair * blk, frames), (((1,), (1,)), ((), ())),
            preferred_element_type=F32,
        )

    def age(i):
        at = pl.ds(pl.multiple_of(i * part, part), part)
        cur[at, :] = cur[at, :] * live

    run(0, pixels // part, age)
    for c, (first, count, low, many) in enumerate(pieces):
        run(1, n_px, lambda k: x_copy(c, k).wait_recv())
        if c < half:
            continue
        if not direct:
            pack = 128 // wid
            for q in range(n_px // pack):
                both = [land[q * pack + j, low : low + many] for j in range(pack)]
                recv[low : low + many, :, q * 128 : (q + 1) * 128] = jnp.concatenate(both, axis=-1)
        run(0, pixels // part, lambda i: cross_part(low, i))

    mine = recv[...].reshape(width, recv.shape[2])
    gram = lax.dot_general(mine, mine, (((1,), (1,)), ((), ())), preferred_element_type=F32)
    eye = lax.broadcasted_iota(jnp.int32, (width, width), 0) == lax.broadcasted_iota(jnp.int32, (width, width), 1)
    denom = jnp.sum(jnp.where(eye, gram, 0.0), axis=0, keepdims=True) + 1e-06 + (1.0 - live)
    inv = 1.0 / denom
    hi, lo = split(jnp.where(eye, 1.0, 0.0) - gram * inv)
    for s in range(slots):
        hilo[s, :, :blk] = hi[:, s * blk : (s + 1) * blk]
        hilo[s, :, blk:] = lo[:, s * blk : (s + 1) * blk]
    def total_copy(step, k):
        dest = lax.rem(me + k, total)
        return pltpu.make_async_remote_copy(
            src_ref=t_send.at[step], dst_ref=t_recv.at[step, k - 1],
            send_sem=t_ssem.at[step], recv_sem=t_rsem.at[step],
            device_id={"py": dest // n_px, "px": lax.rem(dest, n_px)}, device_id_type=MESH,
        )

    ids_f = tile.astype(F32)
    scale = jnp.ones((1, width), F32)
    put = pltpu.make_async_copy(cur, cur_out, local_sem.at[4])
    for step in range(ITERS):

        def sweep(i, sums, scale=scale):
            at = pl.ds(pl.multiple_of(i * part, part), part)
            now = cur[at, :] * scale
            pieces = [now[:, s * blk : (s + 1) * blk] for s in range(slots)]
            his, los = zip(*[split(p) for p in pieces])
            his, los = list(his), list(los)
            squares = []
            for s in range(slots):
                m = hilo[s]
                wide = mm(jnp.concatenate(his, axis=1), m)
                thin = mm(jnp.concatenate(los, axis=1), m[:, :blk])
                fresh = jnp.maximum(
                    crs[at, s * blk : (s + 1) * blk] * inv[:, s * blk : (s + 1) * blk] + (wide[:, :blk] + wide[:, blk:] + thin), 0.0
                )
                cur[at, s * blk : (s + 1) * blk] = fresh
                his[s], los[s] = split(fresh)
                squares.append(jnp.sum(fresh * fresh, axis=0, keepdims=True))
            return sums + jnp.concatenate(squares, axis=1)

        sums = lax.fori_loop(0, pixels // part, sweep, jnp.zeros((1, width), F32))
        mine_tile = ids_f
        for s in range(slots):
            mine_tile = jnp.where(sub == s, sums[:, s * blk : (s + 1) * blk], mine_tile)
        t_send[step] = mine_tile
        run(1, total, lambda k: total_copy(step, k).start())
        if step == ITERS - 1:
            put.start()
        pltpu.make_async_copy(t_recv.at[step], t_recv.at[step], t_rsem.at[step]).wait()
        got = t_recv[step]
        scales = []
        for s in range(slots):
            want = ids_f[4 + s : 5 + s, :]
            acc = sums[:, s * blk : (s + 1) * blk]
            same = jnp.where(got[:, 4 : 4 + slots, :] == want[None], got[:, :slots, :], 0.0)
            acc = acc + jnp.sum(jnp.sum(same, axis=0), axis=0, keepdims=True)
            scales.append(1.0 / jnp.sqrt(acc / (pixels * total) + 1e-06))
        scale = jnp.concatenate(scales, axis=1) * live
    scale_out[...] = jnp.broadcast_to(scale, scale_out.shape)

    put.wait()
    for c in range(CHUNKS):
        run(1, n_py, lambda k: gather_copy(c, k).wait_send())
    for c in range(len(pieces)):
        run(1, n_px, lambda k: x_copy(c, k).wait_send())
    for step in range(ITERS):
        pltpu.make_async_copy(t_recv.at[step], t_recv.at[step], t_ssem.at[step]).wait()


def per_device(n_py, n_px, movie, traces, footprints, block_ids):
    rows, cols, frames = movie.shape
    pixels = rows * cols
    width = footprints.shape[-1]
    slots = block_ids.shape[-1]
    blk = width // slots
    wid = traces.shape[1]
    loc = traces.shape[0] // blk
    total = n_py * n_px
    hbm = pl.BlockSpec(memory_space=pl.ANY)
    dma = pltpu.SemaphoreType.DMA
    current, scale = pl.pallas_call(
        functools.partial(kernel, n_py, n_px),
        out_shape=(
            jax.ShapeDtypeStruct((pixels, width), F32),
            jax.ShapeDtypeStruct((8, width), F32),
        ),
        in_specs=[hbm, hbm, hbm, pl.BlockSpec(memory_space=pltpu.SMEM)],
        out_specs=(hbm, pl.BlockSpec(memory_space=pltpu.VMEM)),
        scratch_shapes=[
            pltpu.VMEM((pixels, frames), BF),
            pltpu.VMEM((n_px, slots, blk, wid), BF),
            pltpu.VMEM((slots, blk, frames), BF),
            pltpu.VMEM((8, 128) if wid % 128 == 0 else (n_px, slots, blk, wid), BF),
            pltpu.VMEM((pixels, width), F32),
            pltpu.VMEM((pixels, width), F32),
            pltpu.VMEM((slots, width, 2 * blk), BF),
            pltpu.VMEM((8, blk), jnp.int32),
            pltpu.VMEM((n_px, 8, blk), jnp.int32),
            pltpu.SMEM((n_px, 8, blk), jnp.int32),
            pltpu.VMEM((ITERS, 8, blk), F32),
            pltpu.VMEM((ITERS, total - 1, 8, blk), F32),
            pltpu.VMEM((1, width), F32),
            dma((5,)), dma((CHUNKS,)),
            dma((n_px,)), dma((n_px,)),
            dma((CHUNKS, n_py)), dma((CHUNKS, n_py)),
            dma((CHUNKS, n_px)), dma((CHUNKS, n_px)),
            dma((ITERS,)), dma((ITERS,)),
            *[pltpu.VMEM((loc * n_py, blk // CHUNKS, wid), BF) for _ in range(CHUNKS)],
        ],
        compiler_params=pltpu.CompilerParams(
            collective_id=0, has_side_effects=True, vmem_limit_bytes=67043328
        ),
    )(
        movie.reshape(pixels, frames),
        traces.reshape(loc, blk, wid),
        footprints.reshape(pixels, width),
        block_ids,
    )
    return (current * scale[:1]).reshape(rows, cols, width)


def solution(mesh):
    return jax.shard_map(
        functools.partial(per_device, mesh.shape["py"], mesh.shape["px"]),
        mesh=mesh,
        in_specs=(P("py", "px", None), P("py", "px"), P("py", "px", None), P("py", "px", None)),
        out_specs=P("py", "px", None),
        check_vma=False,
    )
```

```python
import functools

import jax
import jax.numpy as jnp
from jax import lax
from jax.experimental import pallas as pl
from jax.experimental.pallas import tpu as pltpu
from jax.sharding import PartitionSpec as P

ITERS = 2
CHUNKS = 8
MESH = pl.DeviceIdType.MESH
BF = jnp.bfloat16
F32 = jnp.float32


def split(x):
    hi = x.astype(BF)
    return hi, (x - hi.astype(F32)).astype(BF)


def mm(a, b):
    return lax.dot_general(a, b, (((1,), (0,)), ((), ())), preferred_element_type=F32)


def kernel(
    n_py, n_px, movie, traces, foot, ids, cur_out, scale_out,
    y_buf, outb, recv, land, cur, crs, hilo, id_tile, id_all, id_smem, t_send, t_recv, live_row, gram_buf,
    local_sem, own_sem, id_ssem, id_rsem, g_ssem, g_rsem, x_ssem, x_rsem, t_ssem, t_rsem, *spans,
):
    py, px = lax.axis_index("py"), lax.axis_index("px")
    total = n_py * n_px
    me = py * n_px + px
    loc, blk, wid = traces.shape
    nblk = loc * n_py
    slots = recv.shape[0]
    width = slots * blk
    direct = wid % 128 == 0
    pixels = y_buf.shape[0]
    step_rows = blk // CHUNKS

    owns = [
        pltpu.make_async_copy(
            traces.at[:, pl.ds(c * step_rows, step_rows), :], spans[c].at[pl.ds(py * loc, loc)], own_sem.at[c]
        )
        for c in range(CHUNKS)
    ]
    for own in owns:
        own.start()
    get_foot = pltpu.make_async_copy(foot, cur, local_sem.at[1])
    get_movie = pltpu.make_async_copy(movie, y_buf, local_sem.at[2])

    sub = lax.broadcasted_iota(jnp.int32, (8, blk), 0)
    tile = jnp.zeros((8, blk), jnp.int32)
    for s in range(slots):
        tile = jnp.where(sub == 4 + s, ids[0, 0, s], tile)
    id_tile[...] = tile
    id_all[px] = tile
    for s in range(slots):
        alive = ((tile[4 + s : 5 + s, :] >= 0) & (tile[4 + s : 5 + s, :] < nblk)).astype(F32)
        live_row[:, s * blk : (s + 1) * blk] = alive

    barrier = pltpu.get_barrier_semaphore()

    def greet(k, _):
        dest = lax.rem(me + k, total)
        pl.semaphore_signal(
            barrier, inc=1, device_id={"py": dest // n_px, "px": lax.rem(dest, n_px)}, device_id_type=MESH
        )
        return _

    lax.fori_loop(1, total, greet, 0)
    pl.semaphore_wait(barrier, total - 1)

    def id_copy(k):
        return pltpu.make_async_remote_copy(
            src_ref=id_tile, dst_ref=id_all.at[px], send_sem=id_ssem.at[k], recv_sem=id_rsem.at[k],
            device_id={"px": lax.rem(px + k, n_px)}, device_id_type=MESH,
        )

    def gather_copy(c, k):
        rows = pl.ds(c * step_rows, step_rows)
        return pltpu.make_async_remote_copy(
            src_ref=traces.at[:, rows, :], dst_ref=spans[c].at[pl.ds(py * loc, loc)],
            send_sem=g_ssem.at[c, k], recv_sem=g_rsem.at[c, k],
            device_id={"py": lax.rem(py + k, n_py)}, device_id_type=MESH,
        )

    half = CHUNKS // 2
    pair = max(slots // 2, 1)
    pieces = [(c, 1, 0, slots) for c in range(half)]
    pieces += [(half, CHUNKS - half, s, pair) for s in range(0, slots, pair)]

    def x_copy(c, k):
        first, count, low, many = pieces[c]
        rows = pl.ds(first * step_rows, count * step_rows)
        group = pl.ds(low, many)
        dest = lax.rem(px + k, n_px)
        if direct:
            target = recv.at[group, rows, pl.ds(pl.multiple_of(px * wid, wid), wid)]
        else:
            target = land.at[px, group, rows, :]
        return pltpu.make_async_remote_copy(
            src_ref=outb.at[dest, group, rows, :],
            dst_ref=target,
            send_sem=x_ssem.at[c, k], recv_sem=x_rsem.at[c, k],
            device_id={"px": dest}, device_id_type=MESH,
        )

    def run(lo, hi, fn):
        def body(k, carry):
            fn(k)
            return carry

        lax.fori_loop(lo, hi, body, 0)

    run(1, n_px, lambda k: id_copy(k).start())
    for c in range(CHUNKS):
        run(1, n_py, lambda k: gather_copy(c, k).start())
    get_movie.start()
    get_foot.start()
    run(1, n_px, lambda k: id_copy(k).wait())
    to_smem = pltpu.make_async_copy(id_all, id_smem, local_sem.at[3])
    to_smem.start()
    to_smem.wait()

    def pick(dest, s, c):
        number = id_smem[dest, 4 + s, 0]
        ok = ((number >= 0) & (number < nblk)).astype(F32).astype(BF)
        index = jnp.minimum(jnp.maximum(number, 0), nblk - 1)
        return spans[c][index] * ok

    for c, (first, count, low, many) in enumerate(pieces):
        if low == 0:
            for g in range(first, first + count):
                owns[g].wait()
                run(1, n_py, lambda k: gather_copy(g, k).wait_recv())

        def route(k):
            dest = lax.rem(px + k, n_px)
            for g in range(first, first + count):
                for s in range(low, low + many):
                    outb[dest, s, pl.ds(g * step_rows, step_rows), :] = pick(dest, s, g)
            x_copy(c, k).start()

        run(1, n_px, route)
        for g in range(first, first + count):
            rows = pl.ds(g * step_rows, step_rows)
            for s in range(low, low + many):
                if direct:
                    recv[s, rows, pl.ds(pl.multiple_of(px * wid, wid), wid)] = pick(px, s, g)
                else:
                    land[px, s, rows, :] = pick(px, s, g)

    get_foot.wait()
    get_movie.wait()
    live = live_row[...]
    part = min(pixels, 256)
    frames = recv.shape[2]

    def cross_part(low, i):
        at = pl.ds(pl.multiple_of(i * part, part), part)
        cols = pl.ds(low * blk, pair * blk)
        crs[at, cols] = lax.dot_general(
            y_buf[at, :], recv[low : low + pair].reshape(pair * blk, frames), (((1,), (1,)), ((), ())),
            preferred_element_type=F32,
        )

    def age(i):
        at = pl.ds(pl.multiple_of(i * part, part), part)
        cur[at, :] = cur[at, :] * live

    run(0, pixels // part, age)
    for c, (first, count, low, many) in enumerate(pieces):
        run(1, n_px, lambda k: x_copy(c, k).wait_recv())
        if c < half:
            continue
        if not direct:
            pack = 128 // wid
            for q in range(n_px // pack):
                both = [land[q * pack + j, low : low + many] for j in range(pack)]
                recv[low : low + many, :, q * 128 : (q + 1) * 128] = jnp.concatenate(both, axis=-1)
        run(0, pixels // part, lambda i: cross_part(low, i))
        near = slice(low * blk, (low + many) * blk)
        far = slice(0, (low + many) * blk)
        fresh_rows = lax.dot_general(
            recv[low : low + many].reshape(many * blk, frames), recv[: low + many].reshape((low + many) * blk, frames),
            (((1,), (1,)), ((), ())), preferred_element_type=F32,
        )
        gram_buf[near, far] = fresh_rows
        if low:
            gram_buf[: low * blk, near] = fresh_rows[:, : low * blk].T

    gram = gram_buf[...]
    eye = lax.broadcasted_iota(jnp.int32, (width, width), 0) == lax.broadcasted_iota(jnp.int32, (width, width), 1)
    denom = jnp.sum(jnp.where(eye, gram, 0.0), axis=0, keepdims=True) + 1e-06 + (1.0 - live)
    inv = 1.0 / denom
    hi, lo = split(jnp.where(eye, 1.0, 0.0) - gram * inv)
    for s in range(slots):
        hilo[s, :, :blk] = hi[:, s * blk : (s + 1) * blk]
        hilo[s, :, blk:] = lo[:, s * blk : (s + 1) * blk]
    def total_copy(step, k):
        dest = lax.rem(me + k, total)
        return pltpu.make_async_remote_copy(
            src_ref=t_send.at[step], dst_ref=t_recv.at[step, k - 1],
            send_sem=t_ssem.at[step], recv_sem=t_rsem.at[step],
            device_id={"py": dest // n_px, "px": lax.rem(dest, n_px)}, device_id_type=MESH,
        )

    ids_f = tile.astype(F32)
    scale = jnp.ones((1, width), F32)
    put = pltpu.make_async_copy(cur, cur_out, local_sem.at[4])
    for step in range(ITERS):

        def sweep(i, sums, scale=scale):
            at = pl.ds(pl.multiple_of(i * part, part), part)
            now = cur[at, :] * scale
            pieces = [now[:, s * blk : (s + 1) * blk] for s in range(slots)]
            his, los = zip(*[split(p) for p in pieces])
            his, los = list(his), list(los)
            squares = []
            for s in range(slots):
                m = hilo[s]
                wide = mm(jnp.concatenate(his, axis=1), m)
                thin = mm(jnp.concatenate(los, axis=1), m[:, :blk])
                fresh = jnp.maximum(
                    crs[at, s * blk : (s + 1) * blk] * inv[:, s * blk : (s + 1) * blk] + (wide[:, :blk] + wide[:, blk:] + thin), 0.0
                )
                cur[at, s * blk : (s + 1) * blk] = fresh
                his[s], los[s] = split(fresh)
                squares.append(jnp.sum(fresh * fresh, axis=0, keepdims=True))
            return sums + jnp.concatenate(squares, axis=1)

        sums = lax.fori_loop(0, pixels // part, sweep, jnp.zeros((1, width), F32))
        mine_tile = ids_f
        for s in range(slots):
            mine_tile = jnp.where(sub == s, sums[:, s * blk : (s + 1) * blk], mine_tile)
        t_send[step] = mine_tile
        run(1, total, lambda k: total_copy(step, k).start())
        if step == ITERS - 1:
            put.start()
        pltpu.make_async_copy(t_recv.at[step], t_recv.at[step], t_rsem.at[step]).wait()
        got = t_recv[step]
        scales = []
        for s in range(slots):
            want = ids_f[4 + s : 5 + s, :]
            acc = sums[:, s * blk : (s + 1) * blk]
            same = jnp.where(got[:, 4 : 4 + slots, :] == want[None], got[:, :slots, :], 0.0)
            acc = acc + jnp.sum(jnp.sum(same, axis=0), axis=0, keepdims=True)
            scales.append(1.0 / jnp.sqrt(acc / (pixels * total) + 1e-06))
        scale = jnp.concatenate(scales, axis=1) * live
    scale_out[...] = jnp.broadcast_to(scale, scale_out.shape)

    put.wait()
    for c in range(CHUNKS):
        run(1, n_py, lambda k: gather_copy(c, k).wait_send())
    for c in range(len(pieces)):
        run(1, n_px, lambda k: x_copy(c, k).wait_send())
    for step in range(ITERS):
        pltpu.make_async_copy(t_recv.at[step], t_recv.at[step], t_ssem.at[step]).wait()


def per_device(n_py, n_px, movie, traces, footprints, block_ids):
    rows, cols, frames = movie.shape
    pixels = rows * cols
    width = footprints.shape[-1]
    slots = block_ids.shape[-1]
    blk = width // slots
    wid = traces.shape[1]
    loc = traces.shape[0] // blk
    total = n_py * n_px
    hbm = pl.BlockSpec(memory_space=pl.ANY)
    dma = pltpu.SemaphoreType.DMA
    current, scale = pl.pallas_call(
        functools.partial(kernel, n_py, n_px),
        out_shape=(
            jax.ShapeDtypeStruct((pixels, width), F32),
            jax.ShapeDtypeStruct((8, width), F32),
        ),
        in_specs=[pl.BlockSpec(memory_space=pltpu.HBM)] * 3 + [pl.BlockSpec(memory_space=pltpu.SMEM)],
        out_specs=(hbm, pl.BlockSpec(memory_space=pltpu.VMEM)),
        scratch_shapes=[
            pltpu.VMEM((pixels, frames), BF),
            pltpu.VMEM((n_px, slots, blk, wid), BF),
            pltpu.VMEM((slots, blk, frames), BF),
            pltpu.VMEM((8, 128) if wid % 128 == 0 else (n_px, slots, blk, wid), BF),
            pltpu.VMEM((pixels, width), F32),
            pltpu.VMEM((pixels, width), F32),
            pltpu.VMEM((slots, width, 2 * blk), BF),
            pltpu.VMEM((8, blk), jnp.int32),
            pltpu.VMEM((n_px, 8, blk), jnp.int32),
            pltpu.SMEM((n_px, 8, blk), jnp.int32),
            pltpu.VMEM((ITERS, 8, blk), F32),
            pltpu.VMEM((ITERS, total - 1, 8, blk), F32),
            pltpu.VMEM((1, width), F32),
            pltpu.VMEM((width, width), F32),
            dma((5,)), dma((CHUNKS,)),
            dma((n_px,)), dma((n_px,)),
            dma((CHUNKS, n_py)), dma((CHUNKS, n_py)),
            dma((CHUNKS, n_px)), dma((CHUNKS, n_px)),
            dma((ITERS,)), dma((ITERS,)),
            *[pltpu.VMEM((loc * n_py, blk // CHUNKS, wid), BF) for _ in range(CHUNKS)],
        ],
        compiler_params=pltpu.CompilerParams(
            collective_id=0, has_side_effects=True, vmem_limit_bytes=48 * 1024 * 1024
        ),
    )(
        movie.reshape(pixels, frames),
        traces.reshape(loc, blk, wid),
        footprints.reshape(pixels, width),
        block_ids,
    )
    return (current * scale[:1]).reshape(rows, cols, width)


def solution(mesh):
    return jax.shard_map(
        functools.partial(per_device, mesh.shape["py"], mesh.shape["px"]),
        mesh=mesh,
        in_specs=(P("py", "px", None), P("py", "px"), P("py", "px", None), P("py", "px", None)),
        out_specs=P("py", "px", None),
        check_vma=False,
    )
```

```python
import functools

import jax
import jax.numpy as jnp
from jax import lax
from jax.experimental import pallas as pl
from jax.experimental.pallas import tpu as pltpu
from jax.sharding import PartitionSpec as P

ITERS = 2
CHUNKS = 8
RELAYED = 2
MESH = pl.DeviceIdType.MESH
BF = jnp.bfloat16
F32 = jnp.float32


def split(x):
    hi = x.astype(BF)
    return hi, (x - hi.astype(F32)).astype(BF)


def mm(a, b):
    return lax.dot_general(a, b, (((1,), (0,)), ((), ())), preferred_element_type=F32)


def relayed(n_py, n_px, wid):
    return RELAYED if wid % 128 == 0 and n_px == 2 * n_py and n_py > 2 else 0


def kernel(
    n_py, n_px, movie, traces, foot, ids, cur_out, scale_out,
    y_buf, outb, recv, land, cur, crs, hilo, id_tile, id_all, id_smem, t_send, t_recv, live_row, gram_buf,
    local_sem, own_sem, id_ssem, id_rsem, g_ssem, g_rsem, x_ssem, x_rsem, t_ssem, t_rsem,
    z_buf, p_buf, outp, idp_all, idp_smem, z_sem, p_ssem, p_rsem, q_ssem, q_rsem, idp_ssem, idp_rsem, *spans,
):
    py, px = lax.axis_index("py"), lax.axis_index("px")
    total = n_py * n_px
    me = py * n_px + px
    loc, blk, wid = traces.shape
    nblk = loc * n_py
    slots = recv.shape[0]
    width = slots * blk
    direct = wid % 128 == 0
    pixels = y_buf.shape[0]
    step_rows = blk // CHUNKS
    relay = relayed(n_py, n_px, wid)
    chunks = CHUNKS - relay
    plane = 2 * n_py
    z, core = px // 2, lax.rem(px, 2)
    spot = py * 2 + core
    nz = n_px // 2
    rest = pl.ds(chunks * step_rows, relay * step_rows)

    owns = [
        pltpu.make_async_copy(
            traces.at[:, pl.ds(c * step_rows, step_rows), :], spans[c].at[pl.ds(py * loc, loc)], own_sem.at[c]
        )
        for c in range(chunks)
    ]
    for own in owns:
        own.start()
    if relay:
        own_z = pltpu.make_async_copy(traces.at[:, rest, :], z_buf.at[z], local_sem.at[5])
        own_z.start()
    get_foot = pltpu.make_async_copy(foot, cur, local_sem.at[1])
    get_movie = pltpu.make_async_copy(movie, y_buf, local_sem.at[2])

    sub = lax.broadcasted_iota(jnp.int32, (8, blk), 0)
    tile = jnp.zeros((8, blk), jnp.int32)
    for s in range(slots):
        tile = jnp.where(sub == 4 + s, ids[0, 0, s], tile)
    id_tile[...] = tile
    id_all[px] = tile
    if relay:
        idp_all[spot] = tile
    for s in range(slots):
        alive = ((tile[4 + s : 5 + s, :] >= 0) & (tile[4 + s : 5 + s, :] < nblk)).astype(F32)
        live_row[:, s * blk : (s + 1) * blk] = alive

    barrier = pltpu.get_barrier_semaphore()

    def greet(k, _):
        dest = lax.rem(me + k, total)
        pl.semaphore_signal(
            barrier, inc=1, device_id={"py": dest // n_px, "px": lax.rem(dest, n_px)}, device_id_type=MESH
        )
        return _

    lax.fori_loop(1, total, greet, 0)
    pl.semaphore_wait(barrier, total - 1)

    def id_copy(k):
        return pltpu.make_async_remote_copy(
            src_ref=id_tile, dst_ref=id_all.at[px], send_sem=id_ssem.at[k], recv_sem=id_rsem.at[k],
            device_id={"px": lax.rem(px + k, n_px)}, device_id_type=MESH,
        )

    def gather_copy(c, k):
        rows = pl.ds(c * step_rows, step_rows)
        return pltpu.make_async_remote_copy(
            src_ref=traces.at[:, rows, :], dst_ref=spans[c].at[pl.ds(py * loc, loc)],
            send_sem=g_ssem.at[c, k], recv_sem=g_rsem.at[c, k],
            device_id={"py": lax.rem(py + k, n_py)}, device_id_type=MESH,
        )

    half = chunks // 2
    pair = max(slots // 2, 1)
    pieces = [(c, 1, 0, slots) for c in range(half)]
    pieces += [(half, chunks - half, s, pair) for s in range(0, slots, pair)]

    def x_copy(c, k):
        first, count, low, many = pieces[c]
        rows = pl.ds(first * step_rows, count * step_rows)
        group = pl.ds(low, many)
        dest = lax.rem(px + k, n_px)
        if direct:
            target = recv.at[group, rows, pl.ds(pl.multiple_of(px * wid, wid), wid)]
        else:
            target = land.at[px, group, rows, :]
        return pltpu.make_async_remote_copy(
            src_ref=outb.at[dest, group, rows, :],
            dst_ref=target,
            send_sem=x_ssem.at[c, k], recv_sem=x_rsem.at[c, k],
            device_id={"px": dest}, device_id_type=MESH,
        )

    def run(lo, hi, fn):
        def body(k, carry):
            fn(k)
            return carry

        lax.fori_loop(lo, hi, body, 0)

    def plane_dest(k):
        other = lax.rem(spot + k, plane)
        return other, {"py": other // 2, "px": z * 2 + lax.rem(other, 2)}

    def idp_copy(k):
        return pltpu.make_async_remote_copy(
            src_ref=id_tile, dst_ref=idp_all.at[spot], send_sem=idp_ssem.at[k], recv_sem=idp_rsem.at[k],
            device_id=plane_dest(k)[1], device_id_type=MESH,
        )

    def chain(way, j):
        source = z - j if way == 0 else z + j
        return pltpu.make_async_remote_copy(
            src_ref=z_buf.at[source], dst_ref=z_buf.at[source],
            send_sem=z_sem.at[way, 0, j], recv_sem=z_sem.at[way, 1, j],
            device_id={"px": px + 2 if way == 0 else px - 2}, device_id_type=MESH,
        )

    def chain_sends(way, j):
        return (z - j >= 0) & (z + 1 < nz) if way == 0 else (z + j < nz) & (z - 1 >= 0)

    def chain_start(j):
        for way in range(2):
            pl.when(chain_sends(way, j))(lambda: chain(way, j).start())

    def chain_wait(j):
        for way in range(2):
            source = z - 1 - j if way == 0 else z + 1 + j
            here = source >= 0 if way == 0 else source < nz

            @pl.when(here)
            def _():
                pltpu.make_async_copy(z_buf.at[source], z_buf.at[source], z_sem.at[way, 1, j]).wait()

    def p_copy(k):
        other = lax.rem(py + k, n_py)
        return pltpu.make_async_remote_copy(
            src_ref=z_buf.at[other], dst_ref=p_buf.at[pl.ds(py * loc, loc)],
            send_sem=p_ssem.at[k], recv_sem=p_rsem.at[k], device_id={"py": other}, device_id_type=MESH,
        )

    def q_copy(k):
        other, place = plane_dest(k)
        return pltpu.make_async_remote_copy(
            src_ref=outp.at[other], dst_ref=recv.at[:, rest, pl.ds(pl.multiple_of(spot * wid, wid), wid)],
            send_sem=q_ssem.at[k], recv_sem=q_rsem.at[k], device_id=place, device_id_type=MESH,
        )

    run(1, n_px, lambda k: id_copy(k).start())
    if relay:
        run(1, plane, lambda k: idp_copy(k).start())
        own_z.wait()
        chain_start(0)
    for c in range(chunks):
        run(1, n_py, lambda k: gather_copy(c, k).start())
    get_movie.start()
    get_foot.start()
    run(1, n_px, lambda k: id_copy(k).wait())
    to_smem = pltpu.make_async_copy(id_all, id_smem, local_sem.at[3])
    to_smem.start()
    to_smem.wait()

    if relay:
        run(1, plane, lambda k: idp_copy(k).wait())
        to_plane = pltpu.make_async_copy(idp_all, idp_smem, local_sem.at[6])
        to_plane.start()
        to_plane.wait()

    def pick_plane(dest, s):
        number = idp_smem[dest, 4 + s, 0]
        ok = ((number >= 0) & (number < nblk)).astype(F32).astype(BF)
        return p_buf[jnp.minimum(jnp.maximum(number, 0), nblk - 1)] * ok

    def pick(dest, s, c):
        number = id_smem[dest, 4 + s, 0]
        ok = ((number >= 0) & (number < nblk)).astype(F32).astype(BF)
        index = jnp.minimum(jnp.maximum(number, 0), nblk - 1)
        return spans[c][index] * ok

    own_p = pltpu.make_async_copy(z_buf.at[lax.rem(py, z_buf.shape[0])], p_buf.at[pl.ds(py * loc, loc)], local_sem.at[5])
    moves = nz - 1 if relay else 0
    for c, (first, count, low, many) in enumerate(pieces):
        if c < moves:
            chain_wait(c)
            if c + 1 < moves:
                chain_start(c + 1)
            else:
                own_p.start()
                run(1, n_py, lambda k: p_copy(k).start())
        if low == 0:
            for g in range(first, first + count):
                owns[g].wait()
                run(1, n_py, lambda k: gather_copy(g, k).wait_recv())

        def route(k):
            dest = lax.rem(px + k, n_px)
            for g in range(first, first + count):
                for s in range(low, low + many):
                    outb[dest, s, pl.ds(g * step_rows, step_rows), :] = pick(dest, s, g)
            x_copy(c, k).start()

        run(1, n_px, route)
        for g in range(first, first + count):
            rows = pl.ds(g * step_rows, step_rows)
            for s in range(low, low + many):
                if direct:
                    recv[s, rows, pl.ds(pl.multiple_of(px * wid, wid), wid)] = pick(px, s, g)
                else:
                    land[px, s, rows, :] = pick(px, s, g)

    if relay:
        own_p.wait()
        run(1, n_py, lambda k: p_copy(k).wait_recv())

        def route_plane(k):
            other = lax.rem(spot + k, plane)
            for s in range(slots):
                outp[other, s] = pick_plane(other, s)
            q_copy(k).start()

        run(1, plane, route_plane)
        for s in range(slots):
            recv[s, rest, pl.ds(pl.multiple_of(spot * wid, wid), wid)] = pick_plane(spot, s)

    get_foot.wait()
    get_movie.wait()
    live = live_row[...]
    part = min(pixels, 256)
    frames = recv.shape[2]

    def cross_part(low, i):
        at = pl.ds(pl.multiple_of(i * part, part), part)
        cols = pl.ds(low * blk, pair * blk)
        crs[at, cols] = lax.dot_general(
            y_buf[at, :], recv[low : low + pair].reshape(pair * blk, frames), (((1,), (1,)), ((), ())),
            preferred_element_type=F32,
        )

    def age(i):
        at = pl.ds(pl.multiple_of(i * part, part), part)
        cur[at, :] = cur[at, :] * live

    run(0, pixels // part, age)
    for c, (first, count, low, many) in enumerate(pieces):
        run(1, n_px, lambda k: x_copy(c, k).wait_recv())
        if c < half:
            continue
        if relay and low == 0:
            run(1, plane, lambda k: q_copy(k).wait_recv())
        if not direct:
            pack = 128 // wid
            for q in range(n_px // pack):
                both = [land[q * pack + j, low : low + many] for j in range(pack)]
                recv[low : low + many, :, q * 128 : (q + 1) * 128] = jnp.concatenate(both, axis=-1)
        run(0, pixels // part, lambda i: cross_part(low, i))
        near = slice(low * blk, (low + many) * blk)
        far = slice(0, (low + many) * blk)
        fresh_rows = lax.dot_general(
            recv[low : low + many].reshape(many * blk, frames), recv[: low + many].reshape((low + many) * blk, frames),
            (((1,), (1,)), ((), ())), preferred_element_type=F32,
        )
        gram_buf[near, far] = fresh_rows
        if low:
            gram_buf[: low * blk, near] = fresh_rows[:, : low * blk].T

    gram = gram_buf[...]
    eye = lax.broadcasted_iota(jnp.int32, (width, width), 0) == lax.broadcasted_iota(jnp.int32, (width, width), 1)
    denom = jnp.sum(jnp.where(eye, gram, 0.0), axis=0, keepdims=True) + 1e-06 + (1.0 - live)
    inv = 1.0 / denom
    hi, lo = split(jnp.where(eye, 1.0, 0.0) - gram * inv)
    for s in range(slots):
        hilo[s, :, :blk] = hi[:, s * blk : (s + 1) * blk]
        hilo[s, :, blk:] = lo[:, s * blk : (s + 1) * blk]
    def total_copy(step, k):
        dest = lax.rem(me + k, total)
        return pltpu.make_async_remote_copy(
            src_ref=t_send.at[step], dst_ref=t_recv.at[step, k - 1],
            send_sem=t_ssem.at[step], recv_sem=t_rsem.at[step],
            device_id={"py": dest // n_px, "px": lax.rem(dest, n_px)}, device_id_type=MESH,
        )

    ids_f = tile.astype(F32)
    scale = jnp.ones((1, width), F32)
    put = pltpu.make_async_copy(cur, cur_out, local_sem.at[4])
    for step in range(ITERS):

        def sweep(i, sums, scale=scale):
            at = pl.ds(pl.multiple_of(i * part, part), part)
            now = cur[at, :] * scale
            pieces = [now[:, s * blk : (s + 1) * blk] for s in range(slots)]
            his, los = zip(*[split(p) for p in pieces])
            his, los = list(his), list(los)
            squares = []
            for s in range(slots):
                m = hilo[s]
                wide = mm(jnp.concatenate(his, axis=1), m)
                thin = mm(jnp.concatenate(los, axis=1), m[:, :blk])
                fresh = jnp.maximum(
                    crs[at, s * blk : (s + 1) * blk] * inv[:, s * blk : (s + 1) * blk] + (wide[:, :blk] + wide[:, blk:] + thin), 0.0
                )
                cur[at, s * blk : (s + 1) * blk] = fresh
                his[s], los[s] = split(fresh)
                squares.append(jnp.sum(fresh * fresh, axis=0, keepdims=True))
            return sums + jnp.concatenate(squares, axis=1)

        sums = lax.fori_loop(0, pixels // part, sweep, jnp.zeros((1, width), F32))
        mine_tile = ids_f
        for s in range(slots):
            mine_tile = jnp.where(sub == s, sums[:, s * blk : (s + 1) * blk], mine_tile)
        t_send[step] = mine_tile
        run(1, total, lambda k: total_copy(step, k).start())
        if step == ITERS - 1:
            put.start()
        pltpu.make_async_copy(t_recv.at[step], t_recv.at[step], t_rsem.at[step]).wait()
        got = t_recv[step]
        scales = []
        for s in range(slots):
            want = ids_f[4 + s : 5 + s, :]
            acc = sums[:, s * blk : (s + 1) * blk]
            same = jnp.where(got[:, 4 : 4 + slots, :] == want[None], got[:, :slots, :], 0.0)
            acc = acc + jnp.sum(jnp.sum(same, axis=0), axis=0, keepdims=True)
            scales.append(1.0 / jnp.sqrt(acc / (pixels * total) + 1e-06))
        scale = jnp.concatenate(scales, axis=1) * live
    scale_out[...] = jnp.broadcast_to(scale, scale_out.shape)

    put.wait()
    for c in range(chunks):
        run(1, n_py, lambda k: gather_copy(c, k).wait_send())
    if relay:
        for j in range(moves):
            for way in range(2):
                pl.when(chain_sends(way, j))(lambda: chain(way, j).wait_send())
        run(1, n_py, lambda k: p_copy(k).wait_send())
        run(1, plane, lambda k: q_copy(k).wait_send())
    for c in range(len(pieces)):
        run(1, n_px, lambda k: x_copy(c, k).wait_send())
    for step in range(ITERS):
        pltpu.make_async_copy(t_recv.at[step], t_recv.at[step], t_ssem.at[step]).wait()


def per_device(n_py, n_px, movie, traces, footprints, block_ids):
    rows, cols, frames = movie.shape
    pixels = rows * cols
    width = footprints.shape[-1]
    slots = block_ids.shape[-1]
    blk = width // slots
    wid = traces.shape[1]
    loc = traces.shape[0] // blk
    total = n_py * n_px
    relay = relayed(n_py, n_px, wid)
    part = relay * (blk // CHUNKS) or 16
    hold = n_py if relay else 1
    plane = 2 * hold
    hbm = pl.BlockSpec(memory_space=pl.ANY)
    dma = pltpu.SemaphoreType.DMA
    current, scale = pl.pallas_call(
        functools.partial(kernel, n_py, n_px),
        out_shape=(
            jax.ShapeDtypeStruct((pixels, width), F32),
            jax.ShapeDtypeStruct((8, width), F32),
        ),
        in_specs=[pl.BlockSpec(memory_space=pltpu.HBM)] * 3 + [pl.BlockSpec(memory_space=pltpu.SMEM)],
        out_specs=(hbm, pl.BlockSpec(memory_space=pltpu.VMEM)),
        scratch_shapes=[
            pltpu.VMEM((pixels, frames), BF),
            pltpu.VMEM((n_px, slots, blk, wid), BF),
            pltpu.VMEM((slots, blk, frames), BF),
            pltpu.VMEM((8, 128) if wid % 128 == 0 else (n_px, slots, blk, wid), BF),
            pltpu.VMEM((pixels, width), F32),
            pltpu.VMEM((pixels, width), F32),
            pltpu.VMEM((slots, width, 2 * blk), BF),
            pltpu.VMEM((8, blk), jnp.int32),
            pltpu.VMEM((n_px, 8, blk), jnp.int32),
            pltpu.SMEM((n_px, 8, blk), jnp.int32),
            pltpu.VMEM((ITERS, 8, blk), F32),
            pltpu.VMEM((ITERS, total - 1, 8, blk), F32),
            pltpu.VMEM((1, width), F32),
            pltpu.VMEM((width, width), F32),
            dma((7,)), dma((CHUNKS,)),
            dma((n_px,)), dma((n_px,)),
            dma((CHUNKS, n_py)), dma((CHUNKS, n_py)),
            dma((CHUNKS, n_px)), dma((CHUNKS, n_px)),
            dma((ITERS,)), dma((ITERS,)),
            pltpu.VMEM((hold, loc, part, wid), BF),
            pltpu.VMEM((loc * n_py, part, wid), BF),
            pltpu.VMEM((plane, slots, part, wid), BF),
            pltpu.VMEM((plane, 8, blk), jnp.int32),
            pltpu.SMEM((plane, 8, blk), jnp.int32),
            dma((2, 2, n_px)),
            dma((n_py,)), dma((n_py,)),
            dma((plane,)), dma((plane,)),
            dma((plane,)), dma((plane,)),
            *[pltpu.VMEM((loc * n_py, blk // CHUNKS, wid), BF) for _ in range(CHUNKS - relay)],
        ],
        compiler_params=pltpu.CompilerParams(
            collective_id=0, has_side_effects=True, vmem_limit_bytes=67043328
        ),
    )(
        movie.reshape(pixels, frames),
        traces.reshape(loc, blk, wid),
        footprints.reshape(pixels, width),
        block_ids,
    )
    return (current * scale[:1]).reshape(rows, cols, width)


def solution(mesh):
    return jax.shard_map(
        functools.partial(per_device, mesh.shape["py"], mesh.shape["px"]),
        mesh=mesh,
        in_specs=(P("py", "px", None), P("py", "px"), P("py", "px", None), P("py", "px", None)),
        out_specs=P("py", "px", None),
        check_vma=False,
    )
```

```python
import functools

import jax
import jax.numpy as jnp
from jax import lax
from jax.experimental import pallas as pl
from jax.experimental.pallas import tpu as pltpu
from jax.sharding import PartitionSpec as P

ITERS = 2
CHUNKS = 8
RELAYED = 3
MESH = pl.DeviceIdType.MESH
BF = jnp.bfloat16
F32 = jnp.float32


def split(x):
    hi = x.astype(BF)
    return hi, (x - hi.astype(F32)).astype(BF)


def mm(a, b):
    return lax.dot_general(a, b, (((1,), (0,)), ((), ())), preferred_element_type=F32)


def relayed(n_py, n_px, wid):
    return RELAYED if wid % 128 == 0 and n_px == 2 * n_py and n_py > 2 else 0


def kernel(
    n_py, n_px, movie, traces, foot, ids, cur_out, scale_out,
    y_buf, outb, recv, land, cur, crs, hilo, id_tile, id_all, id_smem, t_send, t_recv, live_row, gram_buf,
    local_sem, own_sem, id_ssem, id_rsem, g_ssem, g_rsem, x_ssem, x_rsem, t_ssem, t_rsem,
    z_buf, p_buf, outp, idp_all, idp_smem, z_sem, p_ssem, p_rsem, q_ssem, q_rsem, idp_ssem, idp_rsem, *spans,
):
    py, px = lax.axis_index("py"), lax.axis_index("px")
    total = n_py * n_px
    me = py * n_px + px
    loc, blk, wid = traces.shape
    nblk = loc * n_py
    slots = recv.shape[0]
    width = slots * blk
    direct = wid % 128 == 0
    pixels = y_buf.shape[0]
    step_rows = blk // CHUNKS
    relay = relayed(n_py, n_px, wid)
    chunks = CHUNKS - relay
    plane = 2 * n_py
    z, core = px // 2, lax.rem(px, 2)
    spot = py * 2 + core
    nz = n_px // 2
    rest = pl.ds(chunks * step_rows, relay * step_rows)

    owns = [
        pltpu.make_async_copy(
            traces.at[:, pl.ds(c * step_rows, step_rows), :], spans[c].at[pl.ds(py * loc, loc)], own_sem.at[c]
        )
        for c in range(chunks)
    ]
    for own in owns:
        own.start()
    if relay:
        own_z = pltpu.make_async_copy(traces.at[:, rest, :], z_buf.at[z], local_sem.at[5])
        own_z.start()
    get_foot = pltpu.make_async_copy(foot, cur, local_sem.at[1])
    get_movie = pltpu.make_async_copy(movie, y_buf, local_sem.at[2])

    sub = lax.broadcasted_iota(jnp.int32, (8, blk), 0)
    tile = jnp.zeros((8, blk), jnp.int32)
    for s in range(slots):
        tile = jnp.where(sub == 4 + s, ids[0, 0, s], tile)
    id_tile[...] = tile
    id_all[px] = tile
    if relay:
        idp_all[spot] = tile
    for s in range(slots):
        alive = ((tile[4 + s : 5 + s, :] >= 0) & (tile[4 + s : 5 + s, :] < nblk)).astype(F32)
        live_row[:, s * blk : (s + 1) * blk] = alive

    barrier = pltpu.get_barrier_semaphore()

    def greet(k, _):
        dest = lax.rem(me + k, total)
        pl.semaphore_signal(
            barrier, inc=1, device_id={"py": dest // n_px, "px": lax.rem(dest, n_px)}, device_id_type=MESH
        )
        return _

    lax.fori_loop(1, total, greet, 0)
    pl.semaphore_wait(barrier, total - 1)

    def id_copy(k):
        return pltpu.make_async_remote_copy(
            src_ref=id_tile, dst_ref=id_all.at[px], send_sem=id_ssem.at[k], recv_sem=id_rsem.at[k],
            device_id={"px": lax.rem(px + k, n_px)}, device_id_type=MESH,
        )

    def gather_copy(c, k):
        rows = pl.ds(c * step_rows, step_rows)
        return pltpu.make_async_remote_copy(
            src_ref=traces.at[:, rows, :], dst_ref=spans[c].at[pl.ds(py * loc, loc)],
            send_sem=g_ssem.at[c, k], recv_sem=g_rsem.at[c, k],
            device_id={"py": lax.rem(py + k, n_py)}, device_id_type=MESH,
        )

    half = chunks // 2
    pair = max(slots // 2, 1)
    pieces = [(c, 1, 0, slots) for c in range(half)]
    pieces += [(half, chunks - half, s, pair) for s in range(0, slots, pair)]

    def x_copy(c, k):
        first, count, low, many = pieces[c]
        rows = pl.ds(first * step_rows, count * step_rows)
        group = pl.ds(low, many)
        dest = lax.rem(px + k, n_px)
        if direct:
            target = recv.at[group, rows, pl.ds(pl.multiple_of(px * wid, wid), wid)]
        else:
            target = land.at[px, group, rows, :]
        return pltpu.make_async_remote_copy(
            src_ref=outb.at[dest, group, rows, :],
            dst_ref=target,
            send_sem=x_ssem.at[c, k], recv_sem=x_rsem.at[c, k],
            device_id={"px": dest}, device_id_type=MESH,
        )

    def run(lo, hi, fn):
        def body(k, carry):
            fn(k)
            return carry

        lax.fori_loop(lo, hi, body, 0)

    def plane_dest(k):
        other = lax.rem(spot + k, plane)
        return other, {"py": other // 2, "px": z * 2 + lax.rem(other, 2)}

    def idp_copy(k):
        return pltpu.make_async_remote_copy(
            src_ref=id_tile, dst_ref=idp_all.at[spot], send_sem=idp_ssem.at[k], recv_sem=idp_rsem.at[k],
            device_id=plane_dest(k)[1], device_id_type=MESH,
        )

    def chain(way, j):
        source = z - j if way == 0 else z + j
        return pltpu.make_async_remote_copy(
            src_ref=z_buf.at[source], dst_ref=z_buf.at[source],
            send_sem=z_sem.at[way, 0, j], recv_sem=z_sem.at[way, 1, j],
            device_id={"px": px + 2 if way == 0 else px - 2}, device_id_type=MESH,
        )

    def chain_sends(way, j):
        return (z - j >= 0) & (z + 1 < nz) if way == 0 else (z + j < nz) & (z - 1 >= 0)

    def chain_start(j):
        for way in range(2):
            pl.when(chain_sends(way, j))(lambda: chain(way, j).start())

    def chain_wait(j):
        for way in range(2):
            source = z - 1 - j if way == 0 else z + 1 + j
            here = source >= 0 if way == 0 else source < nz

            @pl.when(here)
            def _():
                pltpu.make_async_copy(z_buf.at[source], z_buf.at[source], z_sem.at[way, 1, j]).wait()

    def p_copy(k):
        other = lax.rem(py + k, n_py)
        return pltpu.make_async_remote_copy(
            src_ref=z_buf.at[other], dst_ref=p_buf.at[pl.ds(py * loc, loc)],
            send_sem=p_ssem.at[k], recv_sem=p_rsem.at[k], device_id={"py": other}, device_id_type=MESH,
        )

    def q_copy(k):
        other, place = plane_dest(k)
        return pltpu.make_async_remote_copy(
            src_ref=outp.at[other], dst_ref=recv.at[:, rest, pl.ds(pl.multiple_of(spot * wid, wid), wid)],
            send_sem=q_ssem.at[k], recv_sem=q_rsem.at[k], device_id=place, device_id_type=MESH,
        )

    run(1, n_px, lambda k: id_copy(k).start())
    if relay:
        run(1, plane, lambda k: idp_copy(k).start())
        own_z.wait()
        chain_start(0)
    for c in range(chunks):
        run(1, n_py, lambda k: gather_copy(c, k).start())
    get_movie.start()
    get_foot.start()
    run(1, n_px, lambda k: id_copy(k).wait())
    to_smem = pltpu.make_async_copy(id_all, id_smem, local_sem.at[3])
    to_smem.start()
    to_smem.wait()

    if relay:
        run(1, plane, lambda k: idp_copy(k).wait())
        to_plane = pltpu.make_async_copy(idp_all, idp_smem, local_sem.at[6])
        to_plane.start()
        to_plane.wait()

    def pick_plane(dest, s):
        number = idp_smem[dest, 4 + s, 0]
        ok = ((number >= 0) & (number < nblk)).astype(F32).astype(BF)
        return p_buf[jnp.minimum(jnp.maximum(number, 0), nblk - 1)] * ok

    def pick(dest, s, c):
        number = id_smem[dest, 4 + s, 0]
        ok = ((number >= 0) & (number < nblk)).astype(F32).astype(BF)
        index = jnp.minimum(jnp.maximum(number, 0), nblk - 1)
        return spans[c][index] * ok

    own_p = pltpu.make_async_copy(z_buf.at[lax.rem(py, z_buf.shape[0])], p_buf.at[pl.ds(py * loc, loc)], local_sem.at[5])
    moves = nz - 1 if relay else 0
    for c, (first, count, low, many) in enumerate(pieces):
        if c < moves:
            chain_wait(c)
            if c + 1 < moves:
                chain_start(c + 1)
            else:
                own_p.start()
                run(1, n_py, lambda k: p_copy(k).start())
        if low == 0:
            for g in range(first, first + count):
                owns[g].wait()
                run(1, n_py, lambda k: gather_copy(g, k).wait_recv())

        def route(k):
            dest = lax.rem(px + k, n_px)
            for g in range(first, first + count):
                for s in range(low, low + many):
                    outb[dest, s, pl.ds(g * step_rows, step_rows), :] = pick(dest, s, g)
            x_copy(c, k).start()

        run(1, n_px, route)
        for g in range(first, first + count):
            rows = pl.ds(g * step_rows, step_rows)
            for s in range(low, low + many):
                if direct:
                    recv[s, rows, pl.ds(pl.multiple_of(px * wid, wid), wid)] = pick(px, s, g)
                else:
                    land[px, s, rows, :] = pick(px, s, g)

    if relay:
        own_p.wait()
        run(1, n_py, lambda k: p_copy(k).wait_recv())

        def route_plane(k):
            other = lax.rem(spot + k, plane)
            for s in range(slots):
                outp[other, s] = pick_plane(other, s)
            q_copy(k).start()

        run(1, plane, route_plane)
        for s in range(slots):
            recv[s, rest, pl.ds(pl.multiple_of(spot * wid, wid), wid)] = pick_plane(spot, s)

    get_foot.wait()
    get_movie.wait()
    live = live_row[...]
    part = min(pixels, 256)
    frames = recv.shape[2]

    def cross_part(low, i):
        at = pl.ds(pl.multiple_of(i * part, part), part)
        cols = pl.ds(low * blk, pair * blk)
        crs[at, cols] = lax.dot_general(
            y_buf[at, :], recv[low : low + pair].reshape(pair * blk, frames), (((1,), (1,)), ((), ())),
            preferred_element_type=F32,
        )

    def age(i):
        at = pl.ds(pl.multiple_of(i * part, part), part)
        cur[at, :] = cur[at, :] * live

    run(0, pixels // part, age)
    for c, (first, count, low, many) in enumerate(pieces):
        run(1, n_px, lambda k: x_copy(c, k).wait_recv())
        if c < half:
            continue
        if relay and low == 0:
            run(1, plane, lambda k: q_copy(k).wait_recv())
        if not direct:
            pack = 128 // wid
            for q in range(n_px // pack):
                both = [land[q * pack + j, low : low + many] for j in range(pack)]
                recv[low : low + many, :, q * 128 : (q + 1) * 128] = jnp.concatenate(both, axis=-1)
        run(0, pixels // part, lambda i: cross_part(low, i))
        near = slice(low * blk, (low + many) * blk)
        far = slice(0, (low + many) * blk)
        fresh_rows = lax.dot_general(
            recv[low : low + many].reshape(many * blk, frames), recv[: low + many].reshape((low + many) * blk, frames),
            (((1,), (1,)), ((), ())), preferred_element_type=F32,
        )
        gram_buf[near, far] = fresh_rows
        if low:
            gram_buf[: low * blk, near] = fresh_rows[:, : low * blk].T

    gram = gram_buf[...]
    eye = lax.broadcasted_iota(jnp.int32, (width, width), 0) == lax.broadcasted_iota(jnp.int32, (width, width), 1)
    denom = jnp.sum(jnp.where(eye, gram, 0.0), axis=0, keepdims=True) + 1e-06 + (1.0 - live)
    inv = 1.0 / denom
    hi, lo = split(jnp.where(eye, 1.0, 0.0) - gram * inv)
    for s in range(slots):
        hilo[s, :, :blk] = hi[:, s * blk : (s + 1) * blk]
        hilo[s, :, blk:] = lo[:, s * blk : (s + 1) * blk]
    def total_copy(step, k):
        dest = lax.rem(me + k, total)
        return pltpu.make_async_remote_copy(
            src_ref=t_send.at[step], dst_ref=t_recv.at[step, k - 1],
            send_sem=t_ssem.at[step], recv_sem=t_rsem.at[step],
            device_id={"py": dest // n_px, "px": lax.rem(dest, n_px)}, device_id_type=MESH,
        )

    ids_f = tile.astype(F32)
    scale = jnp.ones((1, width), F32)
    put = pltpu.make_async_copy(cur, cur_out, local_sem.at[4])
    for step in range(ITERS):

        def sweep(i, sums, scale=scale):
            at = pl.ds(pl.multiple_of(i * part, part), part)
            now = cur[at, :] * scale
            pieces = [now[:, s * blk : (s + 1) * blk] for s in range(slots)]
            his, los = zip(*[split(p) for p in pieces])
            his, los = list(his), list(los)
            squares = []
            for s in range(slots):
                m = hilo[s]
                wide = mm(jnp.concatenate(his, axis=1), m)
                thin = mm(jnp.concatenate(los, axis=1), m[:, :blk])
                fresh = jnp.maximum(
                    crs[at, s * blk : (s + 1) * blk] * inv[:, s * blk : (s + 1) * blk] + (wide[:, :blk] + wide[:, blk:] + thin), 0.0
                )
                cur[at, s * blk : (s + 1) * blk] = fresh
                his[s], los[s] = split(fresh)
                squares.append(jnp.sum(fresh * fresh, axis=0, keepdims=True))
            return sums + jnp.concatenate(squares, axis=1)

        sums = lax.fori_loop(0, pixels // part, sweep, jnp.zeros((1, width), F32))
        mine_tile = ids_f
        for s in range(slots):
            mine_tile = jnp.where(sub == s, sums[:, s * blk : (s + 1) * blk], mine_tile)
        t_send[step] = mine_tile
        run(1, total, lambda k: total_copy(step, k).start())
        if step == ITERS - 1:
            put.start()
        pltpu.make_async_copy(t_recv.at[step], t_recv.at[step], t_rsem.at[step]).wait()
        got = t_recv[step]
        scales = []
        for s in range(slots):
            want = ids_f[4 + s : 5 + s, :]
            acc = sums[:, s * blk : (s + 1) * blk]
            same = jnp.where(got[:, 4 : 4 + slots, :] == want[None], got[:, :slots, :], 0.0)
            acc = acc + jnp.sum(jnp.sum(same, axis=0), axis=0, keepdims=True)
            scales.append(1.0 / jnp.sqrt(acc / (pixels * total) + 1e-06))
        scale = jnp.concatenate(scales, axis=1) * live
    scale_out[...] = jnp.broadcast_to(scale, scale_out.shape)

    put.wait()
    for c in range(chunks):
        run(1, n_py, lambda k: gather_copy(c, k).wait_send())
    if relay:
        for j in range(moves):
            for way in range(2):
                pl.when(chain_sends(way, j))(lambda: chain(way, j).wait_send())
        run(1, n_py, lambda k: p_copy(k).wait_send())
        run(1, plane, lambda k: q_copy(k).wait_send())
    for c in range(len(pieces)):
        run(1, n_px, lambda k: x_copy(c, k).wait_send())
    for step in range(ITERS):
        pltpu.make_async_copy(t_recv.at[step], t_recv.at[step], t_ssem.at[step]).wait()


def per_device(n_py, n_px, movie, traces, footprints, block_ids):
    rows, cols, frames = movie.shape
    pixels = rows * cols
    width = footprints.shape[-1]
    slots = block_ids.shape[-1]
    blk = width // slots
    wid = traces.shape[1]
    loc = traces.shape[0] // blk
    total = n_py * n_px
    relay = relayed(n_py, n_px, wid)
    part = relay * (blk // CHUNKS) or 16
    hold = n_py if relay else 1
    plane = 2 * hold
    hbm = pl.BlockSpec(memory_space=pl.ANY)
    dma = pltpu.SemaphoreType.DMA
    current, scale = pl.pallas_call(
        functools.partial(kernel, n_py, n_px),
        out_shape=(
            jax.ShapeDtypeStruct((pixels, width), F32),
            jax.ShapeDtypeStruct((8, width), F32),
        ),
        in_specs=[pl.BlockSpec(memory_space=pltpu.HBM)] * 3 + [pl.BlockSpec(memory_space=pltpu.SMEM)],
        out_specs=(hbm, pl.BlockSpec(memory_space=pltpu.VMEM)),
        scratch_shapes=[
            pltpu.VMEM((pixels, frames), BF),
            pltpu.VMEM((n_px, slots, blk, wid), BF),
            pltpu.VMEM((slots, blk, frames), BF),
            pltpu.VMEM((8, 128) if wid % 128 == 0 else (n_px, slots, blk, wid), BF),
            pltpu.VMEM((pixels, width), F32),
            pltpu.VMEM((pixels, width), F32),
            pltpu.VMEM((slots, width, 2 * blk), BF),
            pltpu.VMEM((8, blk), jnp.int32),
            pltpu.VMEM((n_px, 8, blk), jnp.int32),
            pltpu.SMEM((n_px, 8, blk), jnp.int32),
            pltpu.VMEM((ITERS, 8, blk), F32),
            pltpu.VMEM((ITERS, total - 1, 8, blk), F32),
            pltpu.VMEM((1, width), F32),
            pltpu.VMEM((width, width), F32),
            dma((7,)), dma((CHUNKS,)),
            dma((n_px,)), dma((n_px,)),
            dma((CHUNKS, n_py)), dma((CHUNKS, n_py)),
            dma((CHUNKS, n_px)), dma((CHUNKS, n_px)),
            dma((ITERS,)), dma((ITERS,)),
            pltpu.VMEM((hold, loc, part, wid), BF),
            pltpu.VMEM((loc * n_py, part, wid), BF),
            pltpu.VMEM((plane, slots, part, wid), BF),
            pltpu.VMEM((plane, 8, blk), jnp.int32),
            pltpu.SMEM((plane, 8, blk), jnp.int32),
            dma((2, 2, n_px)),
            dma((n_py,)), dma((n_py,)),
            dma((plane,)), dma((plane,)),
            dma((plane,)), dma((plane,)),
            *[pltpu.VMEM((loc * n_py, blk // CHUNKS, wid), BF) for _ in range(CHUNKS - relay)],
        ],
        compiler_params=pltpu.CompilerParams(
            collective_id=0, has_side_effects=True, vmem_limit_bytes=67043328
        ),
    )(
        movie.reshape(pixels, frames),
        traces.reshape(loc, blk, wid),
        footprints.reshape(pixels, width),
        block_ids,
    )
    return (current * scale[:1]).reshape(rows, cols, width)


def solution(mesh):
    return jax.shard_map(
        functools.partial(per_device, mesh.shape["py"], mesh.shape["px"]),
        mesh=mesh,
        in_specs=(P("py", "px", None), P("py", "px"), P("py", "px", None), P("py", "px", None)),
        out_specs=P("py", "px", None),
        check_vma=False,
    )
```

```python
import functools

import jax
import jax.numpy as jnp
from jax import lax
from jax.experimental import pallas as pl
from jax.experimental.pallas import tpu as pltpu
from jax.sharding import PartitionSpec as P

ITERS = 2
CHUNKS = 8
RELAYED = 2
MESH = pl.DeviceIdType.MESH
BF = jnp.bfloat16
F32 = jnp.float32


def split(x):
    hi = x.astype(BF)
    return hi, (x - hi.astype(F32)).astype(BF)


def mm(a, b):
    return lax.dot_general(a, b, (((1,), (0,)), ((), ())), preferred_element_type=F32)


def relayed(n_py, n_px, wid):
    return RELAYED if wid % 128 == 0 and n_px == 2 * n_py and n_py > 2 else 0


def kernel(
    n_py, n_px, movie, traces, foot, ids, cur_out, scale_out,
    y_buf, outb, recv, land, cur, crs, hilo, id_tile, id_all, id_smem, t_send, t_recv, live_row, gram_buf,
    local_sem, own_sem, id_ssem, id_rsem, g_ssem, g_rsem, x_ssem, x_rsem, t_ssem, t_rsem,
    z_buf, p_buf, outp, idp_all, idp_smem, z_sem, p_ssem, p_rsem, q_ssem, q_rsem, idp_ssem, idp_rsem, *spans,
):
    py, px = lax.axis_index("py"), lax.axis_index("px")
    total = n_py * n_px
    me = py * n_px + px
    loc, blk, wid = traces.shape
    nblk = loc * n_py
    slots = recv.shape[0]
    width = slots * blk
    direct = wid % 128 == 0
    pixels = y_buf.shape[0]
    step_rows = blk // CHUNKS
    relay = relayed(n_py, n_px, wid)
    chunks = CHUNKS - relay
    plane = 2 * n_py
    z, core = px // 2, lax.rem(px, 2)
    spot = py * 2 + core
    nz = n_px // 2
    rest = pl.ds(chunks * step_rows, relay * step_rows)

    owns = [
        pltpu.make_async_copy(
            traces.at[:, pl.ds(c * step_rows, step_rows), :], spans[c].at[pl.ds(py * loc, loc)], own_sem.at[c]
        )
        for c in range(chunks)
    ]
    for own in owns:
        own.start()
    if relay:
        own_z = pltpu.make_async_copy(traces.at[:, rest, :], z_buf.at[z], local_sem.at[5])
        own_z.start()
    get_foot = pltpu.make_async_copy(foot, cur, local_sem.at[1])
    get_movie = pltpu.make_async_copy(movie, y_buf, local_sem.at[2])

    sub = lax.broadcasted_iota(jnp.int32, (8, blk), 0)
    tile = jnp.zeros((8, blk), jnp.int32)
    for s in range(slots):
        tile = jnp.where(sub == 4 + s, ids[0, 0, s], tile)
    id_tile[...] = tile
    id_all[px] = tile
    if relay:
        idp_all[spot] = tile
    for s in range(slots):
        alive = ((tile[4 + s : 5 + s, :] >= 0) & (tile[4 + s : 5 + s, :] < nblk)).astype(F32)
        live_row[:, s * blk : (s + 1) * blk] = alive

    barrier = pltpu.get_barrier_semaphore()

    def greet(k, _):
        dest = lax.rem(me + k, total)
        pl.semaphore_signal(
            barrier, inc=1, device_id={"py": dest // n_px, "px": lax.rem(dest, n_px)}, device_id_type=MESH
        )
        return _

    lax.fori_loop(1, total, greet, 0)
    pl.semaphore_wait(barrier, total - 1)

    def id_copy(k):
        return pltpu.make_async_remote_copy(
            src_ref=id_tile, dst_ref=id_all.at[px], send_sem=id_ssem.at[k], recv_sem=id_rsem.at[k],
            device_id={"px": lax.rem(px + k, n_px)}, device_id_type=MESH,
        )

    def gather_copy(c, k):
        rows = pl.ds(c * step_rows, step_rows)
        return pltpu.make_async_remote_copy(
            src_ref=traces.at[:, rows, :], dst_ref=spans[c].at[pl.ds(py * loc, loc)],
            send_sem=g_ssem.at[c, k], recv_sem=g_rsem.at[c, k],
            device_id={"py": lax.rem(py + k, n_py)}, device_id_type=MESH,
        )

    half = chunks // 2
    pair = max(slots // 2, 1)
    pieces = [(c, 1, 0, slots) for c in range(half)]
    pieces += [(half, chunks - half, s, pair) for s in range(0, slots, pair)]

    def x_copy(c, k):
        first, count, low, many = pieces[c]
        rows = pl.ds(first * step_rows, count * step_rows)
        group = pl.ds(low, many)
        dest = lax.rem(px + k, n_px)
        if direct:
            target = recv.at[group, rows, pl.ds(pl.multiple_of(px * wid, wid), wid)]
        else:
            target = land.at[px, group, rows, :]
        return pltpu.make_async_remote_copy(
            src_ref=outb.at[dest, group, rows, :],
            dst_ref=target,
            send_sem=x_ssem.at[c, k], recv_sem=x_rsem.at[c, k],
            device_id={"px": dest}, device_id_type=MESH,
        )

    def run(lo, hi, fn):
        def body(k, carry):
            fn(k)
            return carry

        lax.fori_loop(lo, hi, body, 0)

    def plane_dest(k):
        other = lax.rem(spot + k, plane)
        return other, {"py": other // 2, "px": z * 2 + lax.rem(other, 2)}

    def idp_copy(k):
        return pltpu.make_async_remote_copy(
            src_ref=id_tile, dst_ref=idp_all.at[spot], send_sem=idp_ssem.at[k], recv_sem=idp_rsem.at[k],
            device_id=plane_dest(k)[1], device_id_type=MESH,
        )

    def chain(way, j):
        source = z - j if way == 0 else z + j
        return pltpu.make_async_remote_copy(
            src_ref=z_buf.at[source], dst_ref=z_buf.at[source],
            send_sem=z_sem.at[way, 0, j], recv_sem=z_sem.at[way, 1, j],
            device_id={"px": px + 2 if way == 0 else px - 2}, device_id_type=MESH,
        )

    def chain_sends(way, j):
        return (z - j >= 0) & (z + 1 < nz) if way == 0 else (z + j < nz) & (z - 1 >= 0)

    def chain_start(j):
        for way in range(2):
            pl.when(chain_sends(way, j))(lambda: chain(way, j).start())

    def chain_wait(j):
        for way in range(2):
            source = z - 1 - j if way == 0 else z + 1 + j
            here = source >= 0 if way == 0 else source < nz

            @pl.when(here)
            def _():
                pltpu.make_async_copy(z_buf.at[source], z_buf.at[source], z_sem.at[way, 1, j]).wait()

    def p_copy(k):
        other = lax.rem(py + k, n_py)
        return pltpu.make_async_remote_copy(
            src_ref=z_buf.at[other], dst_ref=p_buf.at[pl.ds(py * loc, loc)],
            send_sem=p_ssem.at[k], recv_sem=p_rsem.at[k], device_id={"py": other}, device_id_type=MESH,
        )

    def q_copy(k):
        other, place = plane_dest(k)
        return pltpu.make_async_remote_copy(
            src_ref=outp.at[other], dst_ref=recv.at[:, rest, pl.ds(pl.multiple_of(spot * wid, wid), wid)],
            send_sem=q_ssem.at[k], recv_sem=q_rsem.at[k], device_id=place, device_id_type=MESH,
        )

    run(1, n_px, lambda k: id_copy(k).start())
    if relay:
        run(1, plane, lambda k: idp_copy(k).start())
        own_z.wait()
        chain_start(0)
    for c in range(chunks):
        run(1, n_py, lambda k: gather_copy(c, k).start())
    get_movie.start()
    get_foot.start()
    run(1, n_px, lambda k: id_copy(k).wait())
    to_smem = pltpu.make_async_copy(id_all, id_smem, local_sem.at[3])
    to_smem.start()
    to_smem.wait()

    if relay:
        run(1, plane, lambda k: idp_copy(k).wait())
        to_plane = pltpu.make_async_copy(idp_all, idp_smem, local_sem.at[6])
        to_plane.start()
        to_plane.wait()

    def pick_plane(dest, s):
        number = idp_smem[dest, 4 + s, 0]
        ok = ((number >= 0) & (number < nblk)).astype(F32).astype(BF)
        return p_buf[jnp.minimum(jnp.maximum(number, 0), nblk - 1)] * ok

    def pick(dest, s, c):
        number = id_smem[dest, 4 + s, 0]
        ok = ((number >= 0) & (number < nblk)).astype(F32).astype(BF)
        index = jnp.minimum(jnp.maximum(number, 0), nblk - 1)
        return spans[c][index] * ok

    own_p = pltpu.make_async_copy(z_buf.at[lax.rem(py, z_buf.shape[0])], p_buf.at[pl.ds(py * loc, loc)], local_sem.at[5])
    moves = nz - 1 if relay else 0
    for c, (first, count, low, many) in enumerate(pieces):
        if c < moves:
            chain_wait(c)
            if c + 1 < moves:
                chain_start(c + 1)
            else:
                own_p.start()
                run(1, n_py, lambda k: p_copy(k).start())
        if low == 0:
            for g in range(first, first + count):
                owns[g].wait()
                run(1, n_py, lambda k: gather_copy(g, k).wait_recv())

        def route(k):
            dest = lax.rem(px + k, n_px)
            for g in range(first, first + count):
                for s in range(low, low + many):
                    outb[dest, s, pl.ds(g * step_rows, step_rows), :] = pick(dest, s, g)
            x_copy(c, k).start()

        run(1, n_px, route)
        for g in range(first, first + count):
            rows = pl.ds(g * step_rows, step_rows)
            for s in range(low, low + many):
                if direct:
                    recv[s, rows, pl.ds(pl.multiple_of(px * wid, wid), wid)] = pick(px, s, g)
                else:
                    land[px, s, rows, :] = pick(px, s, g)

    if relay:
        own_p.wait()
        run(1, n_py, lambda k: p_copy(k).wait_recv())

        def route_plane(k):
            other = lax.rem(spot + k, plane)
            for s in range(slots):
                outp[other, s] = pick_plane(other, s)
            q_copy(k).start()

        run(1, plane, route_plane)
        for s in range(slots):
            recv[s, rest, pl.ds(pl.multiple_of(spot * wid, wid), wid)] = pick_plane(spot, s)

    get_foot.wait()
    get_movie.wait()
    live = live_row[...]
    part = min(pixels, 512)
    frames = recv.shape[2]

    def cross_part(low, i):
        at = pl.ds(pl.multiple_of(i * part, part), part)
        cols = pl.ds(low * blk, pair * blk)
        crs[at, cols] = lax.dot_general(
            y_buf[at, :], recv[low : low + pair].reshape(pair * blk, frames), (((1,), (1,)), ((), ())),
            preferred_element_type=F32,
        )

    def age(i):
        at = pl.ds(pl.multiple_of(i * part, part), part)
        cur[at, :] = cur[at, :] * live

    run(0, pixels // part, age)
    for c, (first, count, low, many) in enumerate(pieces):
        run(1, n_px, lambda k: x_copy(c, k).wait_recv())
        if c < half:
            continue
        if relay and low == 0:
            run(1, plane, lambda k: q_copy(k).wait_recv())
        if not direct:
            pack = 128 // wid
            for q in range(n_px // pack):
                both = [land[q * pack + j, low : low + many] for j in range(pack)]
                recv[low : low + many, :, q * 128 : (q + 1) * 128] = jnp.concatenate(both, axis=-1)
        run(0, pixels // part, lambda i: cross_part(low, i))
        near = slice(low * blk, (low + many) * blk)
        far = slice(0, (low + many) * blk)
        fresh_rows = lax.dot_general(
            recv[low : low + many].reshape(many * blk, frames), recv[: low + many].reshape((low + many) * blk, frames),
            (((1,), (1,)), ((), ())), preferred_element_type=F32,
        )
        gram_buf[near, far] = fresh_rows
        if low:
            gram_buf[: low * blk, near] = fresh_rows[:, : low * blk].T

    gram = gram_buf[...]
    eye = lax.broadcasted_iota(jnp.int32, (width, width), 0) == lax.broadcasted_iota(jnp.int32, (width, width), 1)
    denom = jnp.sum(jnp.where(eye, gram, 0.0), axis=0, keepdims=True) + 1e-06 + (1.0 - live)
    inv = 1.0 / denom
    hi, lo = split(jnp.where(eye, 1.0, 0.0) - gram * inv)
    for s in range(slots):
        hilo[s, :, :blk] = hi[:, s * blk : (s + 1) * blk]
        hilo[s, :, blk:] = lo[:, s * blk : (s + 1) * blk]
    def total_copy(step, k):
        dest = lax.rem(me + k, total)
        return pltpu.make_async_remote_copy(
            src_ref=t_send.at[step], dst_ref=t_recv.at[step, k - 1],
            send_sem=t_ssem.at[step], recv_sem=t_rsem.at[step],
            device_id={"py": dest // n_px, "px": lax.rem(dest, n_px)}, device_id_type=MESH,
        )

    ids_f = tile.astype(F32)
    scale = jnp.ones((1, width), F32)
    put = pltpu.make_async_copy(cur, cur_out, local_sem.at[4])
    for step in range(ITERS):

        def sweep(i, sums, scale=scale):
            at = pl.ds(pl.multiple_of(i * part, part), part)
            now = cur[at, :] * scale
            pieces = [now[:, s * blk : (s + 1) * blk] for s in range(slots)]
            his, los = zip(*[split(p) for p in pieces])
            his, los = list(his), list(los)
            squares = []
            for s in range(slots):
                m = hilo[s]
                wide = mm(jnp.concatenate(his, axis=1), m)
                thin = mm(jnp.concatenate(los, axis=1), m[:, :blk])
                fresh = jnp.maximum(
                    crs[at, s * blk : (s + 1) * blk] * inv[:, s * blk : (s + 1) * blk] + (wide[:, :blk] + wide[:, blk:] + thin), 0.0
                )
                cur[at, s * blk : (s + 1) * blk] = fresh
                his[s], los[s] = split(fresh)
                squares.append(jnp.sum(fresh * fresh, axis=0, keepdims=True))
            return sums + jnp.concatenate(squares, axis=1)

        sums = lax.fori_loop(0, pixels // part, sweep, jnp.zeros((1, width), F32))
        mine_tile = ids_f
        for s in range(slots):
            mine_tile = jnp.where(sub == s, sums[:, s * blk : (s + 1) * blk], mine_tile)
        t_send[step] = mine_tile
        run(1, total, lambda k: total_copy(step, k).start())
        if step == ITERS - 1:
            put.start()
        pltpu.make_async_copy(t_recv.at[step], t_recv.at[step], t_rsem.at[step]).wait()
        got = t_recv[step]
        scales = []
        for s in range(slots):
            want = ids_f[4 + s : 5 + s, :]
            acc = sums[:, s * blk : (s + 1) * blk]
            same = jnp.where(got[:, 4 : 4 + slots, :] == want[None], got[:, :slots, :], 0.0)
            acc = acc + jnp.sum(jnp.sum(same, axis=0), axis=0, keepdims=True)
            scales.append(1.0 / jnp.sqrt(acc / (pixels * total) + 1e-06))
        scale = jnp.concatenate(scales, axis=1) * live
    scale_out[...] = jnp.broadcast_to(scale, scale_out.shape)

    put.wait()
    for c in range(chunks):
        run(1, n_py, lambda k: gather_copy(c, k).wait_send())
    if relay:
        for j in range(moves):
            for way in range(2):
                pl.when(chain_sends(way, j))(lambda: chain(way, j).wait_send())
        run(1, n_py, lambda k: p_copy(k).wait_send())
        run(1, plane, lambda k: q_copy(k).wait_send())
    for c in range(len(pieces)):
        run(1, n_px, lambda k: x_copy(c, k).wait_send())
    for step in range(ITERS):
        pltpu.make_async_copy(t_recv.at[step], t_recv.at[step], t_ssem.at[step]).wait()


def per_device(n_py, n_px, movie, traces, footprints, block_ids):
    rows, cols, frames = movie.shape
    pixels = rows * cols
    width = footprints.shape[-1]
    slots = block_ids.shape[-1]
    blk = width // slots
    wid = traces.shape[1]
    loc = traces.shape[0] // blk
    total = n_py * n_px
    relay = relayed(n_py, n_px, wid)
    part = relay * (blk // CHUNKS) or 16
    hold = n_py if relay else 1
    plane = 2 * hold
    hbm = pl.BlockSpec(memory_space=pl.ANY)
    dma = pltpu.SemaphoreType.DMA
    current, scale = pl.pallas_call(
        functools.partial(kernel, n_py, n_px),
        out_shape=(
            jax.ShapeDtypeStruct((pixels, width), F32),
            jax.ShapeDtypeStruct((8, width), F32),
        ),
        in_specs=[pl.BlockSpec(memory_space=pltpu.HBM)] * 3 + [pl.BlockSpec(memory_space=pltpu.SMEM)],
        out_specs=(hbm, pl.BlockSpec(memory_space=pltpu.VMEM)),
        scratch_shapes=[
            pltpu.VMEM((pixels, frames), BF),
            pltpu.VMEM((n_px, slots, blk, wid), BF),
            pltpu.VMEM((slots, blk, frames), BF),
            pltpu.VMEM((8, 128) if wid % 128 == 0 else (n_px, slots, blk, wid), BF),
            pltpu.VMEM((pixels, width), F32),
            pltpu.VMEM((pixels, width), F32),
            pltpu.VMEM((slots, width, 2 * blk), BF),
            pltpu.VMEM((8, blk), jnp.int32),
            pltpu.VMEM((n_px, 8, blk), jnp.int32),
            pltpu.SMEM((n_px, 8, blk), jnp.int32),
            pltpu.VMEM((ITERS, 8, blk), F32),
            pltpu.VMEM((ITERS, total - 1, 8, blk), F32),
            pltpu.VMEM((1, width), F32),
            pltpu.VMEM((width, width), F32),
            dma((7,)), dma((CHUNKS,)),
            dma((n_px,)), dma((n_px,)),
            dma((CHUNKS, n_py)), dma((CHUNKS, n_py)),
            dma((CHUNKS, n_px)), dma((CHUNKS, n_px)),
            dma((ITERS,)), dma((ITERS,)),
            pltpu.VMEM((hold, loc, part, wid), BF),
            pltpu.VMEM((loc * n_py, part, wid), BF),
            pltpu.VMEM((plane, slots, part, wid), BF),
            pltpu.VMEM((plane, 8, blk), jnp.int32),
            pltpu.SMEM((plane, 8, blk), jnp.int32),
            dma((2, 2, n_px)),
            dma((n_py,)), dma((n_py,)),
            dma((plane,)), dma((plane,)),
            dma((plane,)), dma((plane,)),
            *[pltpu.VMEM((loc * n_py, blk // CHUNKS, wid), BF) for _ in range(CHUNKS - relay)],
        ],
        compiler_params=pltpu.CompilerParams(
            collective_id=0, has_side_effects=True, vmem_limit_bytes=67043328
        ),
    )(
        movie.reshape(pixels, frames),
        traces.reshape(loc, blk, wid),
        footprints.reshape(pixels, width),
        block_ids,
    )
    return (current * scale[:1]).reshape(rows, cols, width)


def solution(mesh):
    return jax.shard_map(
        functools.partial(per_device, mesh.shape["py"], mesh.shape["px"]),
        mesh=mesh,
        in_specs=(P("py", "px", None), P("py", "px"), P("py", "px", None), P("py", "px", None)),
        out_specs=P("py", "px", None),
        check_vma=False,
    )
```
